512 devices in a mesh: dp: 32 (over x, z_lo, core), factor: 16 (over y, z_hi).
Axes of the slice: x: 4, y: 4, z: 16 (z_hi: 4, z_lo: 4; z = z_hi * 4 + z_lo), core: 2. Of those that a mesh axis runs over, the one named last changes fastest.
Arguments:
- attn_in: bfloat16 [32768, 8192], P('dp', 'factor'), may hold values from -21 to 21
- mlp_in: bfloat16 [32768, 8192], P('dp', 'factor'), may hold values from -21 to 21
- attn_hgrad: bfloat16 [32768, 192], P('dp'), may hold values from -6 to 6
- mlp_hgrad: bfloat16 [32768, 128], P('dp'), may hold values from -6 to 6
- attn_basis: bfloat16 [8192, 8192], P('factor', 'dp'), may hold values from -0.0625 to 0.0625
- mlp_basis: bfloat16 [8192, 8192], P('factor', 'dp'), may hold values from -0.0625 to 0.0625
- attn_eig: float32 [8192], P('dp'), may hold values from 0.001 to 0.03
- mlp_eig: float32 [8192], P('dp'), may hold values from 0.001 to 0.03
- rank_basis: float32 [5, 64, 64], replicated, may hold values from -0.75 to 0.75
- rank_eig: float32 [5, 64], replicated, may hold values from 0.3 to 3
Outputs:
- attn_update: float32 [192, 8192], P(None, 'factor')
- mlp_update: float32 [128, 8192], P(None, 'factor')
The draws below stay inside these ranges and needn't reach their ends.
All inputs are finite; a program needn't handle non-finite values.
Results may differ from the reference program's by a relative error of at most 0.0003.
Values sent between devices are 32-bit elements; how exact they have to be, the bound alone decides.
No kernel may reach another device: no remote copies, remote signals or barrier semaphores. Data moves between devices by JAX's collectives and lax.ppermute only.
A program may use at most 64 MiB of HBM per device.

```python
import math
import jax
import jax.numpy as jnp
from jax import lax

D = 8192
R = 64
TOKENS = 32768
CA = 192
CM = 128


def draw_inputs(key):
    column = 1.0 + 2.0 * jnp.arange(D, dtype=jnp.float32) / (D - 1)
    base = jax.random.truncated_normal(key, -4.0, 4.0, (TOKENS, D), jnp.float32)
    return (base * column[None, :]).astype(jnp.bfloat16)


def draw_attn_in(key, part):
    return draw_inputs(jax.random.fold_in(key, 11))


def draw_mlp_in(key, part):
    return draw_inputs(jax.random.fold_in(key, 29))


def level_of(rng, extent, pieces, smallest, top_value):
    level, own = 1.0, jax.random.fold_in(rng, 6)
    for dim, parts in pieces:
        heights = jnp.exp(jax.random.uniform(jax.random.fold_in(own, dim), (parts,), jnp.float32, smallest / len(pieces), top_value / len(pieces)))
        level = level * jnp.repeat(heights, extent[dim] // parts).reshape([-1 if axis == dim else 1 for axis in range(len(extent))])
    return level


def bell_draw(key, shape, deviation, bound, cuts=(), held_as=jnp.bfloat16):
    array = deviation * jax.random.normal(key, shape, jnp.float32)
    if cuts:
        array = array * level_of(key, shape, cuts, -0.22, 0.18)
    return jnp.clip(array, -bound, bound).astype(held_as)


def setup_inputs(seed: int = 0) -> dict:
    key_list = jax.random.split(jax.random.key(seed), 11)
    attn_in = draw_attn_in(jax.random.fold_in(key_list[10], 71), 0)
    mlp_in = draw_mlp_in(jax.random.fold_in(key_list[10], 71), 0)
    attn_hgrad = bell_draw(key_list[2], (TOKENS, CA), 1.0, 6.0, ((0, 32),))
    mlp_hgrad = bell_draw(key_list[3], (TOKENS, CM), 1.0, 6.0, ((0, 32),))
    attn_basis = bell_draw(key_list[4], (D, D), D ** -0.5, 0.0625, ((0, 16), (1, 32)))
    mlp_basis = bell_draw(key_list[5], (D, D), D ** -0.5, 0.0625, ((0, 16), (1, 32)))
    attn_eig = jnp.clip(jnp.exp(math.log(0.03) - 3.4011973 * jax.random.uniform(key_list[6], (D,), jnp.float32) ** level_of(key_list[6], (D,), ((0, 32),), -0.2, 0.2)), 0.001, 0.03)
    mlp_eig = jnp.clip(jnp.exp(math.log(0.03) - 3.4011973 * jax.random.uniform(key_list[7], (D,), jnp.float32) ** level_of(key_list[7], (D,), ((0, 32),), -0.2, 0.2)), 0.001, 0.03)
    rank_basis = bell_draw(key_list[8], (5, R, R), R ** -0.5, 0.75, (), jnp.float32)
    rank_eig = jnp.clip(jnp.exp(jax.random.uniform(key_list[9], (5, R), jnp.float32, math.log(0.3), math.log(3.0))), 0.3, 3.0)
    return {"attn_in": attn_in, "mlp_in": mlp_in, "attn_hgrad": attn_hgrad, "mlp_hgrad": mlp_hgrad, "attn_basis": attn_basis, "mlp_basis": mlp_basis, "attn_eig": attn_eig, "mlp_eig": mlp_eig, "rank_basis": rank_basis, "rank_eig": rank_eig}


damping = 0.001
kl_limit = 8000.0

def rank_rotate(blocks, grad, transpose):
    count = blocks.shape[0]
    rank = blocks.shape[1]
    split = grad.reshape(count, rank, grad.shape[1])
    if transpose:
        out = jnp.einsum('pab,pan->pbn', blocks, split, precision=lax.Precision.HIGHEST)
    else:
        out = jnp.einsum('pab,pbn->pan', blocks, split, precision=lax.Precision.HIGHEST)
    return out.reshape(count * rank, grad.shape[1])

def one_group(inputs, hgrad, basis, eig_in, blocks, eig_out):
    grad = lax.dot_general(hgrad, inputs, (((0,), (0,)), ((), ())), preferred_element_type=jnp.float32) / TOKENS
    pre = rank_rotate(blocks, grad, True)
    wide = basis.astype(jnp.float32)
    rot = jnp.dot(pre, wide, precision=lax.Precision.HIGHEST)
    scaled = rot / (eig_out.reshape(-1)[:, None] * eig_in[None, :] + damping)
    back = jnp.dot(scaled, wide.T, precision=lax.Precision.HIGHEST)
    prec = rank_rotate(blocks, back, False)
    return (prec, grad)

def reference(attn_in, mlp_in, attn_hgrad, mlp_hgrad, attn_basis, mlp_basis, attn_eig, mlp_eig, rank_basis, rank_eig):
    attn_prec, attn_grad = one_group(attn_in, attn_hgrad, attn_basis, attn_eig, rank_basis[:3], rank_eig[:3])
    mlp_prec, mlp_grad = one_group(mlp_in, mlp_hgrad, mlp_basis, mlp_eig, rank_basis[3:], rank_eig[3:])
    quad = jnp.sum(attn_prec * attn_grad) + jnp.sum(mlp_prec * mlp_grad)
    clip = jnp.minimum(jnp.float32(1.0), jnp.sqrt(kl_limit / quad))
    return (clip * attn_prec, clip * mlp_prec)
```

```python
import jax
import jax.numpy as jnp
from jax import lax
from jax.sharding import PartitionSpec as P

damping = 0.001
kl_limit = 8000.0
HI = lax.Precision.HIGHEST

CORE_PAIRS = [[x * 8 + z * 2 + c for c in range(2)] for x in range(4) for z in range(4)]
CHIPS = [[x * 8 + z * 2 + c for x in range(4) for z in range(4)] for c in range(2)]
Y_GROUPS = [[y * 4 + z for y in range(4)] for z in range(4)]
Z_GROUPS = [[y * 4 + z for z in range(4)] for y in range(4)]


def exchange(x, axis, groups):
    return lax.all_to_all(x, axis, 0, 0, axis_index_groups=groups, tiled=True)


def copies(x, count):
    return jnp.broadcast_to(x[None], (count,) + x.shape)


def tiles(x):
    rows, cols = x.shape
    return x.reshape(rows // 8, 8, cols // 128, 128).transpose(0, 2, 1, 3).reshape(-1, 8, 128)


def untile(t, rows, cols):
    return t.reshape(rows // 8, cols // 128, 8, 128).transpose(0, 2, 1, 3).reshape(rows, cols)


def chip_halves(x):
    half = x.shape[1] // 2
    return jnp.stack([tiles(x[:, :half]), tiles(x[:, half:])])


def core_sum(x):
    return jnp.sum(exchange(chip_halves(x), "dp", CORE_PAIRS), axis=0)


def spread(shard, rows, cols):
    own = exchange(copies(shard, 16), "dp", CHIPS).reshape(-1, 8, 128)
    both = lax.all_gather(own, "dp", axis_index_groups=CORE_PAIRS)
    half = cols // 2
    return untile(both[0], rows, half), untile(both[1], rows, half)


def rank_rotate(blocks, x, transpose):
    count, rank = blocks.shape[0], blocks.shape[1]
    split = x.reshape(count, rank, x.shape[1])
    spec = "pab,pan->pbn" if transpose else "pab,pbn->pan"
    return jnp.einsum(spec, blocks, split, precision=HI).reshape(x.shape)


def body(
    attn_in,
    mlp_in,
    attn_hgrad,
    mlp_hgrad,
    attn_basis,
    mlp_basis,
    attn_eig,
    mlp_eig,
    rank_basis,
    rank_eig,
):
    total_tokens = attn_in.shape[0] * lax.axis_size("dp")
    ca, cm = attn_hgrad.shape[1], mlp_hgrad.shape[1]
    rows, feats, cols = ca + cm, attn_in.shape[1], attn_basis.shape[1]
    half = feats // 2
    contract0 = (((0,), (0,)), ((), ()))
    attn_part = lax.dot_general(attn_hgrad, attn_in, contract0, preferred_element_type=jnp.float32)
    mlp_part = lax.dot_general(mlp_hgrad, mlp_in, contract0, preferred_element_type=jnp.float32)
    part = jnp.concatenate([attn_part, mlp_part]) / total_tokens

    shard = exchange(core_sum(part).reshape(16, -1, 8, 128), "dp", CHIPS)
    lo, hi = spread(jnp.sum(shard, axis=0), rows, feats)
    wide_a, wide_m = attn_basis.astype(jnp.float32), mlp_basis.astype(jnp.float32)

    def rotate(g_lo, g_hi, wide):
        out = jnp.dot(g_lo, wide[:half], precision=HI)
        return out + jnp.dot(g_hi, wide[half:], precision=HI)

    rot_part = jnp.concatenate([rotate(lo[:ca], hi[:ca], wide_a), rotate(lo[ca:], hi[ca:], wide_m)])
    rot_part = rank_rotate(rank_basis, rot_part, True)

    block = jnp.sum(exchange(tiles(rot_part).reshape(4, -1, 8, 128), "factor", Y_GROUPS), axis=0)
    block = jnp.sum(exchange(copies(block, 4), "factor", Z_GROUPS), axis=0)
    y = lax.axis_index("factor") // 4
    rot = untile(block, rows // 4, cols)
    eig_rows = jnp.concatenate([jnp.broadcast_to(attn_eig, (ca, cols)), jnp.broadcast_to(mlp_eig, (cm, cols))])
    denominator = rank_eig.reshape(-1)[:, None] * eig_rows + damping
    scaled = rot / lax.dynamic_slice(denominator, (y * (rows // 4), 0), (rows // 4, cols))
    quad = jnp.broadcast_to(jnp.sum(scaled * rot), (1, 8, 128))
    sent = jnp.concatenate([tiles(scaled), quad])
    got = exchange(copies(sent, 4), "factor", Y_GROUPS)
    quad = jnp.sum(got[:, -1, 0, 0])
    scaled = untile(got[:, :-1].reshape(-1, 8, 128), rows, cols)
    scaled = rank_rotate(rank_basis, scaled, False)

    contract1 = (((1,), (1,)), ((), ()))
    back_part = jnp.concatenate(
        [
            lax.dot_general(scaled[:ca], wide_a, contract1, precision=HI),
            lax.dot_general(scaled[ca:], wide_m, contract1, precision=HI),
        ]
    )
    quad_tile = jnp.broadcast_to(quad, (2, 1, 8, 128))
    halves = jnp.concatenate([chip_halves(back_part), quad_tile], axis=1)
    summed = jnp.sum(exchange(halves, "dp", CORE_PAIRS), axis=0)
    sent = jnp.concatenate([summed[:-1].reshape(16, -1, 8, 128), copies(summed[-1:], 16)], axis=1)
    summed = jnp.sum(exchange(sent, "dp", CHIPS), axis=0)
    clip = jnp.minimum(jnp.float32(1.0), jnp.sqrt(kl_limit / summed[-1]))
    lo, hi = spread(clip * summed[:-1], rows, feats)
    update = jnp.concatenate([lo, hi], axis=1)
    return (update[:ca], update[ca:])


def solution(mesh):
    in_specs = (
        P("dp", "factor"),
        P("dp", "factor"),
        P("dp", None),
        P("dp", None),
        P("factor", "dp"),
        P("factor", "dp"),
        P("dp"),
        P("dp"),
        P(),
        P(),
    )
    out_specs = (P(None, "factor"), P(None, "factor"))
    return jax.shard_map(body, mesh=mesh, in_specs=in_specs, out_specs=out_specs, check_vma=False)
```

```python
import jax
import jax.numpy as jnp
from jax import lax
from jax.sharding import PartitionSpec as P

damping = 0.001
kl_limit = 8000.0
HI = lax.Precision.HIGHEST

CORE_PAIRS = [[x * 8 + z * 2 + c for c in range(2)] for x in range(4) for z in range(4)]
CHIPS = [[x * 8 + z * 2 + c for x in range(4) for z in range(4)] for c in range(2)]
Y_GROUPS = [[y * 4 + z for y in range(4)] for z in range(4)]
Z_GROUPS = [[y * 4 + z for z in range(4)] for y in range(4)]


def exchange(x, axis, groups):
    return lax.all_to_all(x, axis, 0, 0, axis_index_groups=groups, tiled=True)


def copies(x, count):
    return jnp.broadcast_to(x[None], (count,) + x.shape)


def tiles(x):
    rows, cols = x.shape
    return x.reshape(rows // 8, 8, cols // 128, 128).transpose(0, 2, 1, 3).reshape(-1, 8, 128)


def untile(t, rows, cols):
    return t.reshape(rows // 8, cols // 128, 8, 128).transpose(0, 2, 1, 3).reshape(rows, cols)


def chip_halves(x):
    half = x.shape[1] // 2
    return jnp.stack([tiles(x[:, :half]), tiles(x[:, half:])])


def core_sum(x):
    return jnp.sum(exchange(chip_halves(x), "dp", CORE_PAIRS), axis=0)


def spread(shard, rows, cols):
    own = exchange(copies(shard, 16), "dp", CHIPS).reshape(-1, 8, 128)
    both = lax.all_gather(own, "dp", axis_index_groups=CORE_PAIRS)
    half = cols // 2
    return untile(both[0], rows, half), untile(both[1], rows, half)


def rank_rotate(blocks, x, transpose):
    count, rank = blocks.shape[0], blocks.shape[1]
    split = x.reshape(count, rank, x.shape[1])
    spec = "pab,pan->pbn" if transpose else "pab,pbn->pan"
    return jnp.einsum(spec, blocks, split, precision=HI).reshape(x.shape)


def to_rotated(inputs, hgrad, basis, eig_in, blocks, eig_out):
    total_tokens = inputs.shape[0] * lax.axis_size("dp")
    rows, feats, cols = hgrad.shape[1], inputs.shape[1], basis.shape[1]
    half = feats // 2
    contract0 = (((0,), (0,)), ((), ()))
    part = lax.dot_general(hgrad, inputs, contract0, preferred_element_type=jnp.float32) / total_tokens
    shard = exchange(core_sum(part).reshape(16, -1, 8, 128), "dp", CHIPS)
    lo, hi = spread(jnp.sum(shard, axis=0), rows, feats)
    wide = basis.astype(jnp.float32)
    rot_part = jnp.dot(lo, wide[:half], precision=HI) + jnp.dot(hi, wide[half:], precision=HI)
    rot_part = rank_rotate(blocks, rot_part, True)
    block = jnp.sum(exchange(tiles(rot_part).reshape(4, -1, 8, 128), "factor", Y_GROUPS), axis=0)
    block = jnp.sum(exchange(copies(block, 4), "factor", Z_GROUPS), axis=0)
    y = lax.axis_index("factor") >> 2
    rot = untile(block, rows // 4, cols)
    eig_rows = lax.dynamic_slice(eig_out.reshape(-1), (y * (rows // 4),), (rows // 4,))
    scaled = rot / (eig_rows[:, None] * eig_in[None, :] + damping)
    quad = jnp.broadcast_to(jnp.sum(scaled * rot), (1, 8, 128))
    sent = jnp.concatenate([tiles(scaled), quad])
    got = exchange(copies(sent, 4), "factor", Y_GROUPS)
    scaled = untile(got[:, :-1].reshape(-1, 8, 128), rows, cols)
    scaled = rank_rotate(blocks, scaled, False)
    contract1 = (((1,), (1,)), ((), ()))
    return lax.dot_general(scaled, wide, contract1, precision=HI), jnp.sum(got[:, -1], axis=0)


def body(
    attn_in,
    mlp_in,
    attn_hgrad,
    mlp_hgrad,
    attn_basis,
    mlp_basis,
    attn_eig,
    mlp_eig,
    rank_basis,
    rank_eig,
):
    attn_back, attn_quad = to_rotated(attn_in, attn_hgrad, attn_basis, attn_eig, rank_basis[:3], rank_eig[:3])
    mlp_back, mlp_quad = to_rotated(mlp_in, mlp_hgrad, mlp_basis, mlp_eig, rank_basis[3:], rank_eig[3:])
    shard = exchange(core_sum(attn_back).reshape(16, -1, 8, 128), "dp", CHIPS)
    attn_lo, attn_hi = spread(jnp.sum(shard, axis=0), *attn_back.shape)

    quad_tile = jnp.broadcast_to(attn_quad + mlp_quad, (2, 1, 8, 128))
    halves = jnp.concatenate([chip_halves(mlp_back), quad_tile], axis=1)
    summed = jnp.sum(exchange(halves, "dp", CORE_PAIRS), axis=0)
    sent = jnp.concatenate([summed[:-1].reshape(16, -1, 8, 128), copies(summed[-1:], 16)], axis=1)
    summed = jnp.sum(exchange(sent, "dp", CHIPS), axis=0)
    clip = jnp.minimum(jnp.float32(1.0), jnp.sqrt(kl_limit / summed[-1, 0, 0]))
    mlp_lo, mlp_hi = spread(summed[:-1], *mlp_back.shape)
    return (
        clip * jnp.concatenate([attn_lo, attn_hi], axis=1),
        clip * jnp.concatenate([mlp_lo, mlp_hi], axis=1),
    )


def solution(mesh):
    in_specs = (
        P("dp", "factor"),
        P("dp", "factor"),
        P("dp", None),
        P("dp", None),
        P("factor", "dp"),
        P("factor", "dp"),
        P("dp"),
        P("dp"),
        P(),
        P(),
    )
    out_specs = (P(None, "factor"), P(None, "factor"))
    return jax.shard_map(body, mesh=mesh, in_specs=in_specs, out_specs=out_specs, check_vma=False)
```

```python
import jax
import jax.numpy as jnp
from jax import lax
from jax.sharding import PartitionSpec as P

damping = 0.001
kl_limit = 8000.0
HI = lax.Precision.HIGHEST

CORE_PAIRS = [[x * 8 + z * 2 + c for c in range(2)] for x in range(4) for z in range(4)]
CHIPS = [[x * 8 + z * 2 + c for x in range(4) for z in range(4)] for c in range(2)]
Y_GROUPS = [[y * 4 + z for y in range(4)] for z in range(4)]
Z_GROUPS = [[y * 4 + z for z in range(4)] for y in range(4)]


def exchange(x, axis, groups):
    return lax.all_to_all(x, axis, 0, 0, axis_index_groups=groups, tiled=True)


def copies(x, count):
    return jnp.broadcast_to(x[None], (count,) + x.shape)


def tiles(x):
    rows, cols = x.shape
    return x.reshape(rows // 8, 8, cols // 128, 128).transpose(0, 2, 1, 3).reshape(-1, 8, 128)


def untile(t, rows, cols):
    return t.reshape(rows // 8, cols // 128, 8, 128).transpose(0, 2, 1, 3).reshape(rows, cols)


def rank_rotate(blocks, x, transpose):
    count, rank = blocks.shape[0], blocks.shape[1]
    split = x.reshape(count, rank, x.shape[1])
    spec = "pab,pan->pbn" if transpose else "pab,pbn->pan"
    return jnp.einsum(spec, blocks, split, precision=HI).reshape(x.shape)


def deal(attn, mlp, parts):
    ca, cm = attn.shape[0] // parts, mlp.shape[0] // parts
    return [
        jnp.concatenate([attn[p * ca : (p + 1) * ca], mlp[p * cm : (p + 1) * cm]]) for p in range(parts)
    ]


def body(
    attn_in,
    mlp_in,
    attn_hgrad,
    mlp_hgrad,
    attn_basis,
    mlp_basis,
    attn_eig,
    mlp_eig,
    rank_basis,
    rank_eig,
):
    total_tokens = attn_in.shape[0] * lax.axis_size("dp")
    ca, cm = attn_hgrad.shape[1], mlp_hgrad.shape[1]
    rows, feats, cols = ca + cm, attn_in.shape[1], attn_basis.shape[1]
    ca2, rows2, rows8 = ca // 2, rows // 2, rows // 8

    wide = jnp.concatenate(
        [
            attn_basis.astype(jnp.float32),
            mlp_basis.astype(jnp.float32),
            jnp.broadcast_to(attn_eig, (8, cols)),
            jnp.broadcast_to(mlp_eig, (8, cols)),
        ]
    )
    swap = [(i, i ^ 1) for i in range(lax.axis_size("dp"))]
    wide = jnp.concatenate([wide, lax.ppermute(wide, "dp", swap)], axis=1)
    wide_a, wide_m = wide[:feats], wide[feats : 2 * feats]

    contract0 = (((0,), (0,)), ((), ()))
    attn_part = lax.dot_general(attn_hgrad, attn_in, contract0, preferred_element_type=jnp.float32)
    mlp_part = lax.dot_general(mlp_hgrad, mlp_in, contract0, preferred_element_type=jnp.float32)
    attn_part = rank_rotate(rank_basis[:3], attn_part / total_tokens, True)
    mlp_part = rank_rotate(rank_basis[3:], mlp_part / total_tokens, True)

    halves = jnp.stack([tiles(h) for h in deal(attn_part, mlp_part, 2)])
    shard = jnp.sum(exchange(halves, "dp", CORE_PAIRS), axis=0)
    shard = jnp.sum(exchange(shard.reshape(16, -1, 8, 128), "dp", CHIPS), axis=0)
    pre = untile(exchange(copies(shard, 16), "dp", CHIPS), rows2, feats)

    rot_a = jnp.dot(pre[:ca2], wide_a, precision=HI)
    rot_m = jnp.dot(pre[ca2:], wide_m, precision=HI)
    block = jnp.stack([tiles(b) for b in deal(rot_a, rot_m, 4)])
    block = jnp.sum(exchange(block, "factor", Y_GROUPS), axis=0)
    block = jnp.sum(exchange(copies(block, 4), "factor", Z_GROUPS), axis=0)
    rot = untile(block, rows8, 2 * cols)
    order = jnp.stack(deal(*[e.reshape(-1) for e in (rank_eig[:3], rank_eig[3:])], 8))
    place = (lax.axis_index("dp") & 1) * 4 + (lax.axis_index("factor") >> 2)
    eig_out = lax.dynamic_slice(order, (place, 0), (1, rows8)).reshape(-1, 1)
    eig_in = jnp.concatenate([jnp.tile(wide[2 * feats : 2 * feats + 8], (ca // 64, 1)), jnp.tile(wide[2 * feats + 8 :], (cm // 64, 1))])
    scaled = rot / (eig_out * eig_in + damping)
    quad = jnp.broadcast_to(jnp.sum(scaled * rot), (1, 8, 128))
    got = exchange(copies(jnp.concatenate([tiles(scaled), quad]), 4), "factor", Y_GROUPS)
    quad = jnp.sum(got[:, -1:], axis=0)
    scaled = untile(got[:, :-1], rows2, 2 * cols).reshape(4, rows8, 2 * cols)
    scaled_a = scaled[:, : ca // 8].reshape(ca2, 2 * cols)
    scaled_m = scaled[:, ca // 8 :].reshape(cm // 2, 2 * cols)

    contract1 = (((1,), (1,)), ((), ()))
    back_a = lax.dot_general(scaled_a, wide_a, contract1, precision=HI)
    back_m = lax.dot_general(scaled_m, wide_m, contract1, precision=HI)
    back = tiles(jnp.concatenate([back_a, back_m])).reshape(16, -1, 8, 128)
    sent = jnp.concatenate([back, copies(quad, 16)], axis=1)
    summed = jnp.sum(exchange(sent, "dp", CHIPS), axis=0)
    back = exchange(copies(summed[:-1], 16), "dp", CHIPS).reshape(-1, 8, 128)
    both = lax.all_gather(jnp.concatenate([back, summed[-1:]]), "dp", axis_index_groups=CORE_PAIRS)
    clip = jnp.minimum(jnp.float32(1.0), jnp.sqrt(kl_limit / (both[0, -1, 0, 0] + both[1, -1, 0, 0])))
    back = [untile(b[:-1], rows2, feats) for b in both]
    attn_back = jnp.concatenate([b[:ca2] for b in back])
    mlp_back = jnp.concatenate([b[ca2:] for b in back])
    return (clip * rank_rotate(rank_basis[:3], attn_back, False), clip * rank_rotate(rank_basis[3:], mlp_back, False))


def solution(mesh):
    in_specs = (
        P("dp", "factor"),
        P("dp", "factor"),
        P("dp", None),
        P("dp", None),
        P("factor", "dp"),
        P("factor", "dp"),
        P("dp"),
        P("dp"),
        P(),
        P(),
    )
    out_specs = (P(None, "factor"), P(None, "factor"))
    return jax.shard_map(body, mesh=mesh, in_specs=in_specs, out_specs=out_specs, check_vma=False)
```

```python
import functools

import jax
import jax.numpy as jnp
from jax import lax
from jax.experimental import pallas as pl
from jax.experimental.pallas import tpu as pltpu
from jax.sharding import PartitionSpec as P


damping = 0.001
kl_limit = 8000.0
HI = lax.Precision.HIGHEST
F32, BF16 = jnp.float32, jnp.bfloat16

CORE_PAIRS = [[x * 8 + z * 2 + c for c in range(2)] for x in range(4) for z in range(4)]
CHIPS = [[x * 8 + z * 2 + c for x in range(4) for z in range(4)] for c in range(2)]
Y_GROUPS = [[y * 4 + z for y in range(4)] for z in range(4)]
Z_GROUPS = [[y * 4 + z for z in range(4)] for y in range(4)]

CA, CM, R = 192, 128, 64
ROWS, HALF_A, HALF_M = CA + CM, CA // 2, CM // 2
HALF = HALF_A + HALF_M
Y_A, Y_M = HALF_A // 4, HALF_M // 4
TOK_STEPS = 4


def exchange(x, axis, groups):
    return lax.all_to_all(x, axis, 0, 0, axis_index_groups=groups, tiled=True)


def copies(x, count):
    return jnp.broadcast_to(x[None], (count,) + x.shape)


def shape(*dims, dtype=F32):
    return pltpu.VMEM(dims, dtype)


def far(*arrays):
    return [pltpu.with_memory_space_constraint(a, pltpu.HBM) for a in arrays]


def near(*arrays):
    return [pltpu.with_memory_space_constraint(a, pltpu.VMEM) for a in arrays]


LIMIT = pltpu.CompilerParams(vmem_limit_bytes=12 * 2**20)
VMEM = pl.BlockSpec(memory_space=pltpu.VMEM)


def pieces(x):
    a = x.astype(BF16)
    r = x - a.astype(F32)
    b = r.astype(BF16)
    c = (r - b.astype(F32)).astype(BF16)
    return jnp.concatenate([a, b, c], axis=0)


def exact_dot(x, basis, contract):
    n = x.shape[0]
    out = lax.dot_general(pieces(x), basis, (((1,), (contract,)), ((), ())), preferred_element_type=F32)
    return (out[2 * n :] + out[n : 2 * n]) + out[:n]


def grad_kernel(scale, a_in, m_in, a_h, m_h, a_b, m_b, a_eig, m_eig, q, send, keep, wide, acc, halves):
    step = pl.program_id(0)
    part_a = lax.dot_general(a_h[...], a_in[...], (((1,), (0,)), ((), ())), preferred_element_type=F32)
    part_m = lax.dot_general(m_h[...], m_in[...], (((0,), (0,)), ((), ())), preferred_element_type=F32)

    @pl.when(step == 0)
    def _():
        acc[:CA] = part_a
        acc[CA:] = part_m
        feats, cols = a_b.shape
        t = 0
        for basis in (a_b, m_b):
            for r in range(0, feats, 16):
                block = basis[r : r + 16].astype(F32)
                for i in range(2):
                    for c in range(cols // 128):
                        wide[t] = block[i * 8 : i * 8 + 8, c * 128 : c * 128 + 128]
                        t += 1
        for eig in (a_eig, m_eig):
            for c in range(cols // 128):
                wide[t] = jnp.broadcast_to(eig[:, c * 128 : c * 128 + 128], (8, 128))
                t += 1

    @pl.when(step > 0)
    def _():
        acc[:CA] += part_a
        acc[CA:] += part_m

    @pl.when(step == pl.num_programs(0) - 1)
    def _():
        cts = acc.shape[1] // 128
        for p in range(ROWS // R):
            g = acc[p * R : (p + 1) * R] * scale
            g = lax.dot_general(q[p], g, (((0,), (0,)), ((), ())), precision=HI, preferred_element_type=F32)
            for i in range(R // 8):
                row = p * R + i * 8
                if row < CA:
                    half, local = divmod(row, HALF_A)
                else:
                    half, local = divmod(row - CA, HALF_M)
                    local += HALF_A
                for c in range(cts):
                    halves[half, local // 8 * cts + c] = g[i * 8 : i * 8 + 8, c * 128 : c * 128 + 128]
        core = lax.axis_index("dp") % 2
        send[...] = halves[1 - core]
        keep[...] = halves[core]


def core_add_kernel(keep, both, out):
    core = lax.axis_index("dp") % 2
    out[...] = keep[...] + both[1 - core]


def rows_of(tiles, rows, first=0):
    cts = tiles.shape[0] // (HALF // 8)
    return jnp.concatenate(
        [
            jnp.concatenate([tiles[(first + r) * cts + c] for c in range(cts)], axis=1)
            for r in range(rows // 8)
        ]
    )


def spread_kernel(got, out):
    total = (got[0] + got[1]) + (got[2] + got[3])
    for k in range(out.shape[0]):
        out[k] = total


def rotate_kernel(pre, own, other, out, basis):
    feats, cols = basis.shape[0] // 2, basis.shape[1] // 2
    cts = cols // 128
    for side, source in enumerate((own, other)):
        for r in range(0, 2 * feats, 16):
            t = r // 8 * cts
            for c in range(cts):
                pair = jnp.concatenate([source[t + c], source[t + cts + c]])
                basis[r : r + 16, (side * cts + c) * 128 : (side * cts + c + 1) * 128] = pair.astype(BF16)
    rot_a = exact_dot(rows_of(pre, HALF_A), basis[:feats], 0)
    rot_m = exact_dot(rows_of(pre, HALF_M, HALF_A // 8), basis[feats:], 0)
    cts = 2 * cts
    for y in range(4):
        for rot, count, first, base in ((rot_a, Y_A // 8, y * Y_A, 0), (rot_m, Y_M // 8, y * Y_M, Y_A // 8)):
            for i in range(count):
                row = first + i * 8
                for c in range(cts):
                    out[y, (base + i) * cts + c] = rot[row : row + 8, c * 128 : c * 128 + 128]


def scale_kernel(got, own, other, eig, out):
    core = lax.axis_index("dp") % 2
    y = lax.axis_index("factor") // 4
    cts = got.shape[1] // ((Y_A + Y_M) // 8)
    eigs = own.shape[0] - cts
    lane = lax.broadcasted_iota(jnp.int32, (8, R), 1)
    sub = lax.broadcasted_iota(jnp.int32, (8, R), 0)
    quad = jnp.zeros((8, 128), F32)
    for rt in range((Y_A + Y_M) // 8):
        if rt < Y_A // 8:
            row, tail = core * HALF_A + y * Y_A + rt * 8, 0
        else:
            row, tail = CA + core * HALF_M + y * Y_M + (rt - Y_A // 8) * 8, cts // 2
        values = jnp.broadcast_to(eig[pl.ds(row // R, 1), :], (8, R))
        col = jnp.sum(jnp.where(lane == sub + row % R, values, 0.0), axis=1, keepdims=True)
        for c in range(cts):
            t = rt * cts + c
            rot = (got[0, t] + got[1, t]) + (got[2, t] + got[3, t])
            source = own if c < cts // 2 else other
            scaled = rot / (col * source[eigs + tail + c % (cts // 2)] + damping)
            quad += scaled * rot
            for k in range(4):
                out[k, t] = scaled
    for k in range(4):
        out[k, out.shape[1] - 1] = quad


def back_kernel(got, basis, out):
    feats = basis.shape[0] // 2
    cts = basis.shape[1] // 128

    def gather(count, base):
        return jnp.concatenate(
            [
                jnp.concatenate([got[y, (base + i) * cts + c] for c in range(cts)], axis=1)
                for y in range(4)
                for i in range(count)
            ]
        )

    back_a = exact_dot(gather(Y_A // 8, 0), basis[:feats], 1)
    back_m = exact_dot(gather(Y_M // 8, Y_A // 8), basis[feats:], 1)
    fts = feats // 128
    per = HALF // 8 * fts // 16
    for back, count, base in ((back_a, HALF_A // 8, 0), (back_m, HALF_M // 8, HALF_A // 8)):
        for i in range(count):
            for c in range(fts):
                t = (base + i) * fts + c
                out[t // per, t % per] = back[i * 8 : i * 8 + 8, c * 128 : c * 128 + 128]
    last = got.shape[1] - 1
    quad = (got[0, last] + got[1, last]) + (got[2, last] + got[3, last])
    for k in range(16):
        out[k, per] = quad


def final_kernel(both, q, attn, mlp):
    per = both.shape[2] - 1
    fts = attn.shape[1] // 128
    quad = jnp.sum(both[0, 0, per] + both[1, 0, per], keepdims=True)
    clip = jnp.minimum(1.0, jnp.sqrt(kl_limit / quad))
    for p in range(ROWS // R):
        rows = []
        for i in range(R // 8):
            row = p * R + i * 8
            if row < CA:
                half, local = divmod(row, HALF_A)
            else:
                half, local = divmod(row - CA, HALF_M)
                local += HALF_A
            ts = [local // 8 * fts + c for c in range(fts)]
            rows.append(jnp.concatenate([both[half, t // per, t % per] for t in ts], axis=1))
        b = jnp.concatenate(rows)
        b = clip * lax.dot_general(q[p], b, (((1,), (0,)), ((), ())), precision=HI, preferred_element_type=F32)
        if p * R < CA:
            attn[p * R : (p + 1) * R] = b
        else:
            mlp[p * R - CA : (p + 1) * R - CA] = b


def body(
    attn_in,
    mlp_in,
    attn_hgrad,
    mlp_hgrad,
    attn_basis,
    mlp_basis,
    attn_eig,
    mlp_eig,
    rank_basis,
    rank_eig,
):
    tokens, feats = attn_in.shape
    cols = attn_basis.shape[1]
    scale = 1.0 / (tokens * lax.axis_size("dp"))
    half_tiles = HALF // 8 * feats // 128
    y_tiles = HALF // 32 * 2 * cols // 128
    chunk = tokens // TOK_STEPS

    def whole(*dims):
        return pl.BlockSpec(dims, lambda i: (0,) * len(dims))

    basis_tiles = 2 * (feats + 8) // 8 * cols // 128
    send, keep, wide = pl.pallas_call(
        functools.partial(grad_kernel, scale),
        grid=(TOK_STEPS,),
        in_specs=[
            pl.BlockSpec((chunk, feats), lambda i: (i, 0)),
            pl.BlockSpec((chunk, feats), lambda i: (i, 0)),
            pl.BlockSpec((CA, chunk), lambda i: (0, i)),
            pl.BlockSpec((chunk, CM), lambda i: (i, 0)),
            whole(feats, cols),
            whole(feats, cols),
            whole(1, cols),
            whole(1, cols),
            whole(5, R, R),
        ],
        out_specs=[whole(half_tiles, 8, 128), whole(half_tiles, 8, 128), whole(basis_tiles, 8, 128)],
        out_shape=[shape(half_tiles, 8, 128), shape(half_tiles, 8, 128), shape(basis_tiles, 8, 128)],
        scratch_shapes=[pltpu.VMEM((ROWS, feats), F32), pltpu.VMEM((2, half_tiles, 8, 128), F32)],
        compiler_params=LIMIT,
        name="grad",
    )(
        *far(
            attn_in,
            mlp_in,
            attn_hgrad.T,
            mlp_hgrad,
            attn_basis,
            mlp_basis,
            attn_eig.reshape(1, -1),
            mlp_eig.reshape(1, -1),
            rank_basis,
        )
    )
    other = lax.ppermute(wide, "dp", [(i, i ^ 1) for i in range(lax.axis_size("dp"))])
    both = lax.all_gather(send, "dp", axis_index_groups=CORE_PAIRS)
    part = pl.pallas_call(
        core_add_kernel,
        in_specs=[VMEM] * 2,
        out_specs=VMEM,
        out_shape=shape(half_tiles, 8, 128),
        compiler_params=LIMIT,
        name="core_add",
    )(*near(keep, both))
    shard, other = lax.optimization_barrier((exchange(part.reshape(16, -1, 8, 128), "dp", CHIPS), other))
    shard = jnp.sum(shard, axis=0)
    pre = exchange(copies(shard, 16), "dp", CHIPS).reshape(-1, 8, 128)

    block, basis = pl.pallas_call(
        rotate_kernel,
        in_specs=[VMEM] * 3,
        out_specs=[VMEM] * 2,
        out_shape=[shape(4, y_tiles, 8, 128), shape(2 * feats, 2 * cols, dtype=BF16)],
        compiler_params=LIMIT,
        name="rotate",
    )(*near(pre, wide, other))
    block = pl.pallas_call(
        spread_kernel,
        in_specs=[VMEM],
        out_specs=VMEM,
        out_shape=shape(4, y_tiles, 8, 128),
        compiler_params=LIMIT,
        name="spread",
    )(*near(exchange(block, "factor", Y_GROUPS)))
    block = exchange(block, "factor", Z_GROUPS)
    scaled = pl.pallas_call(
        scale_kernel,
        in_specs=[VMEM] * 4,
        out_specs=VMEM,
        out_shape=shape(4, y_tiles + 1, 8, 128),
        compiler_params=LIMIT,
        name="scale",
    )(*near(block, wide, other, rank_eig))
    scaled = exchange(scaled, "factor", Y_GROUPS)
    back = pl.pallas_call(
        back_kernel,
        in_specs=[VMEM] * 2,
        out_specs=VMEM,
        out_shape=shape(16, half_tiles // 16 + 1, 8, 128),
        compiler_params=LIMIT, name="back",
    )(*near(scaled, basis))
    summed = jnp.sum(exchange(back, "dp", CHIPS), axis=0)
    back = exchange(copies(summed, 16), "dp", CHIPS)
    both = lax.all_gather(back, "dp", axis_index_groups=CORE_PAIRS)
    return tuple(
        pl.pallas_call(
            final_kernel,
            in_specs=[VMEM] * 2,
            out_specs=[VMEM] * 2,
            out_shape=[jax.ShapeDtypeStruct((CA, feats), F32), jax.ShapeDtypeStruct((CM, feats), F32)],
            compiler_params=LIMIT, name="final",
        )(*near(both, rank_basis))
    )


def solution(mesh):
    in_specs = (
        P("dp", "factor"),
        P("dp", "factor"),
        P("dp", None),
        P("dp", None),
        P("factor", "dp"),
        P("factor", "dp"),
        P("dp"),
        P("dp"),
        P(),
        P(),
    )
    out_specs = (P(None, "factor"), P(None, "factor"))


    return jax.shard_map(body, mesh=mesh, in_specs=in_specs, out_specs=out_specs, check_vma=False)
```

```python
import functools

import jax
import jax.numpy as jnp
from jax import lax
from jax.experimental import pallas as pl
from jax.experimental.pallas import tpu as pltpu
from jax.sharding import PartitionSpec as P


damping = 0.001
kl_limit = 8000.0
HI = lax.Precision.HIGHEST
F32, BF16 = jnp.float32, jnp.bfloat16

CORE_PAIRS = [[x * 8 + z * 2 + c for c in range(2)] for x in range(4) for z in range(4)]
CHIPS = [[x * 8 + z * 2 + c for x in range(4) for z in range(4)] for c in range(2)]
Y_GROUPS = [[y * 4 + z for y in range(4)] for z in range(4)]
Z_PAIRS = [(y * 4 + z, y * 4 + (z ^ 1)) for y in range(4) for z in range(4)]
Z_CROSS = [(y * 4 + z, y * 4 + 3 - z) for y in range(4) for z in range(4)]

CA, CM, R = 192, 128, 64
ROWS, HALF_A, HALF_M = CA + CM, CA // 2, CM // 2
HALF = HALF_A + HALF_M
Y_A, Y_M = HALF_A // 4, HALF_M // 4
TOK_STEPS = 1


def exchange(x, axis, groups):
    return lax.all_to_all(x, axis, 0, 0, axis_index_groups=groups, tiled=True)


def copies(x, count):
    return jnp.broadcast_to(x[None], (count,) + x.shape)


def shape(*dims, dtype=F32):
    return pltpu.VMEM(dims, dtype)


def far(*arrays):
    return [pltpu.with_memory_space_constraint(a, pltpu.HBM) for a in arrays]


def near(*arrays):
    return [pltpu.with_memory_space_constraint(a, pltpu.VMEM) for a in arrays]


LIMIT = pltpu.CompilerParams(vmem_limit_bytes=12 * 2**20)
VMEM = pl.BlockSpec(memory_space=pltpu.VMEM)


def pieces(x):
    a = x.astype(BF16)
    r = x - a.astype(F32)
    b = r.astype(BF16)
    c = (r - b.astype(F32)).astype(BF16)
    return jnp.concatenate([a, b, c], axis=0)


def exact_dot(x, basis, contract):
    n = x.shape[0]
    out = lax.dot_general(pieces(x), basis, (((1,), (contract,)), ((), ())), preferred_element_type=F32)
    return (out[2 * n :] + out[n : 2 * n]) + out[:n]


def grad_kernel(scale, a_in, m_in, a_h, m_h, a_b, m_b, a_eig, m_eig, q, send, keep, wide, acc, halves):
    step = pl.program_id(0)
    part_a = lax.dot_general(a_h[...], a_in[...], (((1,), (0,)), ((), ())), preferred_element_type=F32)
    part_m = lax.dot_general(m_h[...], m_in[...], (((0,), (0,)), ((), ())), preferred_element_type=F32)

    @pl.when(step == 0)
    def _():
        acc[:CA] = part_a
        acc[CA:] = part_m
        feats, cols = a_b.shape
        t = 0
        for basis in (a_b, m_b):
            for r in range(0, feats, 16):
                block = basis[r : r + 16].astype(F32)
                for i in range(2):
                    for c in range(cols // 128):
                        wide[t] = block[i * 8 : i * 8 + 8, c * 128 : c * 128 + 128]
                        t += 1
        for eig in (a_eig, m_eig):
            for c in range(cols // 128):
                wide[t] = jnp.broadcast_to(eig[:, c * 128 : c * 128 + 128], (8, 128))
                t += 1

    @pl.when(step > 0)
    def _():
        acc[:CA] += part_a
        acc[CA:] += part_m

    @pl.when(step == pl.num_programs(0) - 1)
    def _():
        cts = acc.shape[1] // 128
        for p in range(ROWS // R):
            g = acc[p * R : (p + 1) * R] * scale
            g = lax.dot_general(q[p], g, (((0,), (0,)), ((), ())), precision=HI, preferred_element_type=F32)
            for i in range(R // 8):
                row = p * R + i * 8
                if row < CA:
                    half, local = divmod(row, HALF_A)
                else:
                    half, local = divmod(row - CA, HALF_M)
                    local += HALF_A
                for c in range(cts):
                    halves[half, local // 8 * cts + c] = g[i * 8 : i * 8 + 8, c * 128 : c * 128 + 128]
        core = lax.axis_index("dp") % 2
        send[...] = halves[1 - core]
        keep[...] = halves[core]


def core_add_kernel(keep, both, out):
    core = lax.axis_index("dp") % 2
    out[...] = keep[...] + both[1 - core]


def rows_of(tiles, rows, first=0):
    cts = tiles.shape[0] // (HALF // 8)
    return jnp.concatenate(
        [
            jnp.concatenate([tiles[(first + r) * cts + c] for c in range(cts)], axis=1)
            for r in range(rows // 8)
        ]
    )


def sum_kernel(got, out):
    out[...] = (got[0] + got[1]) + (got[2] + got[3])


def add_kernel(one, two, out):
    out[...] = one[...] + two[...]


def rotate_kernel(pre, own, other, out, basis):
    feats, cols = basis.shape[0] // 2, basis.shape[1] // 2
    cts = cols // 128
    for side, source in enumerate((own, other)):
        for r in range(0, 2 * feats, 16):
            t = r // 8 * cts
            for c in range(cts):
                pair = jnp.concatenate([source[t + c], source[t + cts + c]])
                basis[r : r + 16, (side * cts + c) * 128 : (side * cts + c + 1) * 128] = pair.astype(BF16)
    rot_a = exact_dot(rows_of(pre, HALF_A), basis[:feats], 0)
    rot_m = exact_dot(rows_of(pre, HALF_M, HALF_A // 8), basis[feats:], 0)
    cts = 2 * cts
    for y in range(4):
        for rot, count, first, base in ((rot_a, Y_A // 8, y * Y_A, 0), (rot_m, Y_M // 8, y * Y_M, Y_A // 8)):
            for i in range(count):
                row = first + i * 8
                for c in range(cts):
                    out[y, (base + i) * cts + c] = rot[row : row + 8, c * 128 : c * 128 + 128]


def scale_kernel(one, two, own, other, eig, out):
    core = lax.axis_index("dp") % 2
    y = lax.axis_index("factor") // 4
    cts = one.shape[0] // ((Y_A + Y_M) // 8)
    eigs = own.shape[0] - cts
    lane = lax.broadcasted_iota(jnp.int32, (8, R), 1)
    sub = lax.broadcasted_iota(jnp.int32, (8, R), 0)
    quad = jnp.zeros((8, 128), F32)
    for rt in range((Y_A + Y_M) // 8):
        if rt < Y_A // 8:
            row, tail = core * HALF_A + y * Y_A + rt * 8, 0
        else:
            row, tail = CA + core * HALF_M + y * Y_M + (rt - Y_A // 8) * 8, cts // 2
        values = jnp.broadcast_to(eig[pl.ds(row // R, 1), :], (8, R))
        col = jnp.sum(jnp.where(lane == sub + row % R, values, 0.0), axis=1, keepdims=True)
        for c in range(cts):
            t = rt * cts + c
            rot = one[t] + two[t]
            source = own if c < cts // 2 else other
            scaled = rot / (col * source[eigs + tail + c % (cts // 2)] + damping)
            quad += scaled * rot
            for k in range(4):
                out[k, t] = scaled
    for k in range(4):
        out[k, out.shape[1] - 1] = quad


def back_kernel(got, basis, out):
    feats = basis.shape[0] // 2
    cts = basis.shape[1] // 128

    def gather(count, base):
        return jnp.concatenate(
            [
                jnp.concatenate([got[y, (base + i) * cts + c] for c in range(cts)], axis=1)
                for y in range(4)
                for i in range(count)
            ]
        )

    back_a = exact_dot(gather(Y_A // 8, 0), basis[:feats], 1)
    back_m = exact_dot(gather(Y_M // 8, Y_A // 8), basis[feats:], 1)
    fts = feats // 128
    per = HALF // 8 * fts // 16
    for back, count, base in ((back_a, HALF_A // 8, 0), (back_m, HALF_M // 8, HALF_A // 8)):
        for i in range(count):
            for c in range(fts):
                t = (base + i) * fts + c
                out[t // per, t % per] = back[i * 8 : i * 8 + 8, c * 128 : c * 128 + 128]
    last = got.shape[1] - 1
    quad = (got[0, last] + got[1, last]) + (got[2, last] + got[3, last])
    for k in range(16):
        out[k, per] = quad


def final_kernel(both, q, attn, mlp):
    per = both.shape[2] - 1
    fts = attn.shape[1] // 128
    quad = jnp.sum(both[0, 0, per] + both[1, 0, per], keepdims=True)
    clip = jnp.minimum(1.0, jnp.sqrt(kl_limit / quad))
    for p in range(ROWS // R):
        rows = []
        for i in range(R // 8):
            row = p * R + i * 8
            if row < CA:
                half, local = divmod(row, HALF_A)
            else:
                half, local = divmod(row - CA, HALF_M)
                local += HALF_A
            ts = [local // 8 * fts + c for c in range(fts)]
            rows.append(jnp.concatenate([both[half, t // per, t % per] for t in ts], axis=1))
        b = jnp.concatenate(rows)
        b = clip * lax.dot_general(q[p], b, (((1,), (0,)), ((), ())), precision=HI, preferred_element_type=F32)
        if p * R < CA:
            attn[p * R : (p + 1) * R] = b
        else:
            mlp[p * R - CA : (p + 1) * R - CA] = b


def body(
    attn_in,
    mlp_in,
    attn_hgrad,
    mlp_hgrad,
    attn_basis,
    mlp_basis,
    attn_eig,
    mlp_eig,
    rank_basis,
    rank_eig,
):
    tokens, feats = attn_in.shape
    cols = attn_basis.shape[1]
    scale = 1.0 / (tokens * lax.axis_size("dp"))
    half_tiles = HALF // 8 * feats // 128
    y_tiles = HALF // 32 * 2 * cols // 128
    chunk = tokens // TOK_STEPS

    def whole(*dims):
        return pl.BlockSpec(dims, lambda i: (0,) * len(dims))

    basis_tiles = 2 * (feats + 8) // 8 * cols // 128
    send, keep, wide = pl.pallas_call(
        functools.partial(grad_kernel, scale),
        grid=(TOK_STEPS,),
        in_specs=[
            pl.BlockSpec((chunk, feats), lambda i: (i, 0)),
            pl.BlockSpec((chunk, feats), lambda i: (i, 0)),
            pl.BlockSpec((CA, chunk), lambda i: (0, i)),
            pl.BlockSpec((chunk, CM), lambda i: (i, 0)),
            whole(feats, cols),
            whole(feats, cols),
            whole(1, cols),
            whole(1, cols),
            whole(5, R, R),
        ],
        out_specs=[whole(half_tiles, 8, 128), whole(half_tiles, 8, 128), whole(basis_tiles, 8, 128)],
        out_shape=[shape(half_tiles, 8, 128), shape(half_tiles, 8, 128), shape(basis_tiles, 8, 128)],
        scratch_shapes=[pltpu.VMEM((ROWS, feats), F32), pltpu.VMEM((2, half_tiles, 8, 128), F32)],
        compiler_params=LIMIT,
        name="grad",
    )(
        *far(
            attn_in,
            mlp_in,
            attn_hgrad.T,
            mlp_hgrad,
            attn_basis,
            mlp_basis,
            attn_eig.reshape(1, -1),
            mlp_eig.reshape(1, -1),
            rank_basis,
        )
    )
    other = lax.ppermute(wide, "dp", [(i, i ^ 1) for i in range(lax.axis_size("dp"))])
    both = lax.all_gather(send, "dp", axis_index_groups=CORE_PAIRS)
    part = pl.pallas_call(
        core_add_kernel,
        in_specs=[VMEM] * 2,
        out_specs=VMEM,
        out_shape=shape(half_tiles, 8, 128),
        compiler_params=LIMIT,
        name="core_add",
    )(*near(keep, both))
    shard, other = lax.optimization_barrier((exchange(part.reshape(16, -1, 8, 128), "dp", CHIPS), other))
    shard = jnp.sum(shard, axis=0)
    pre = exchange(copies(shard, 16), "dp", CHIPS).reshape(-1, 8, 128)

    block, basis = pl.pallas_call(
        rotate_kernel,
        in_specs=[VMEM] * 3,
        out_specs=[VMEM] * 2,
        out_shape=[shape(4, y_tiles, 8, 128), shape(2 * feats, 2 * cols, dtype=BF16)],
        compiler_params=LIMIT,
        name="rotate",
    )(*near(pre, wide, other))
    block = pl.pallas_call(
        sum_kernel,
        in_specs=[VMEM],
        out_specs=VMEM,
        out_shape=shape(y_tiles, 8, 128),
        compiler_params=LIMIT,
        name="y_sum",
    )(*near(exchange(block, "factor", Y_GROUPS)))
    block = pl.pallas_call(
        add_kernel,
        in_specs=[VMEM] * 2,
        out_specs=VMEM,
        out_shape=shape(y_tiles, 8, 128),
        compiler_params=LIMIT,
        name="z_add",
    )(*near(block, lax.ppermute(block, "factor", Z_PAIRS)))
    across = lax.ppermute(block, "factor", Z_CROSS)
    scaled = pl.pallas_call(
        scale_kernel,
        in_specs=[VMEM] * 5,
        out_specs=VMEM,
        out_shape=shape(4, y_tiles + 1, 8, 128),
        compiler_params=LIMIT,
        name="scale",
    )(*near(block, across, wide, other, rank_eig))
    scaled = exchange(scaled, "factor", Y_GROUPS)
    back = pl.pallas_call(
        back_kernel,
        in_specs=[VMEM] * 2,
        out_specs=VMEM,
        out_shape=shape(16, half_tiles // 16 + 1, 8, 128),
        compiler_params=LIMIT, name="back",
    )(*near(scaled, basis))
    summed = jnp.sum(exchange(back, "dp", CHIPS), axis=0)
    back = exchange(copies(summed, 16), "dp", CHIPS)
    both = lax.all_gather(back, "dp", axis_index_groups=CORE_PAIRS)
    return tuple(
        pl.pallas_call(
            final_kernel,
            in_specs=[VMEM] * 2,
            out_specs=[VMEM] * 2,
            out_shape=[jax.ShapeDtypeStruct((CA, feats), F32), jax.ShapeDtypeStruct((CM, feats), F32)],
            compiler_params=LIMIT, name="final",
        )(*near(both, rank_basis))
    )


def solution(mesh):
    in_specs = (
        P("dp", "factor"),
        P("dp", "factor"),
        P("dp", None),
        P("dp", None),
        P("factor", "dp"),
        P("factor", "dp"),
        P("dp"),
        P("dp"),
        P(),
        P(),
    )
    out_specs = (P(None, "factor"), P(None, "factor"))


    return jax.shard_map(body, mesh=mesh, in_specs=in_specs, out_specs=out_specs, check_vma=False)
```

```python
import functools

import jax
import jax.numpy as jnp
from jax import lax
from jax.experimental import pallas as pl
from jax.experimental.pallas import tpu as pltpu
from jax.sharding import PartitionSpec as P


damping = 0.001
kl_limit = 8000.0
HI = lax.Precision.HIGHEST
F32, BF16 = jnp.float32, jnp.bfloat16

CORE_PAIRS = [[x * 8 + z * 2 + c for c in range(2)] for x in range(4) for z in range(4)]
CHIPS = [[x * 8 + z * 2 + c for x in range(4) for z in range(4)] for c in range(2)]
Y_GROUPS = [[y * 4 + z for y in range(4)] for z in range(4)]
Z_PAIRS = [(y * 4 + z, y * 4 + (z ^ 1)) for y in range(4) for z in range(4)]
Z_CROSS = [(y * 4 + z, y * 4 + 3 - z) for y in range(4) for z in range(4)]

CA, CM, R = 192, 128, 64
ROWS, HALF_A, HALF_M = CA + CM, CA // 2, CM // 2
HALF = HALF_A + HALF_M
Y_A, Y_M = HALF_A // 4, HALF_M // 4


def exchange(x, axis, groups):
    return lax.all_to_all(x, axis, 0, 0, axis_index_groups=groups, tiled=True)


def copies(x, count):
    return jnp.broadcast_to(x[None], (count,) + x.shape)


def shape(*dims, dtype=F32):
    return pltpu.VMEM(dims, dtype)


def far(*arrays):
    return [pltpu.with_memory_space_constraint(a, pltpu.HBM) for a in arrays]


def near(*arrays):
    return [pltpu.with_memory_space_constraint(a, pltpu.VMEM) for a in arrays]


LIMIT = pltpu.CompilerParams(vmem_limit_bytes=12 * 2**20)
VMEM = pl.BlockSpec(memory_space=pltpu.VMEM)
HBM = pl.BlockSpec(memory_space=pltpu.HBM)


def pieces(x):
    a = x.astype(BF16)
    r = x - a.astype(F32)
    b = r.astype(BF16)
    c = (r - b.astype(F32)).astype(BF16)
    return jnp.concatenate([a, b, c], axis=0)


def exact_dot(x, basis, contract):
    n = x.shape[0]
    out = lax.dot_general(pieces(x), basis, (((1,), (contract,)), ((), ())), preferred_element_type=F32)
    return (out[2 * n :] + out[n : 2 * n]) + out[:n]


def grad_kernel(scale, *refs):
    sources, (send, keep, wide), landed = refs[:9], refs[9:12], refs[12:21]
    halves, arrived = refs[21:]
    loads = [pltpu.make_async_copy(s, d, arrived.at[i]) for i, (s, d) in enumerate(zip(sources, landed))]
    for load in loads:
        load.start()
    a_b, m_b, a_eig, m_eig, q, a_h, a_in, m_h, m_in = landed
    feats, cols = a_b.shape
    t = 0
    for i, basis in enumerate((a_b, m_b)):
        loads[i].wait()
        for r in range(0, feats, 16):
            block = basis[r : r + 16].astype(F32)
            for k in range(2):
                for c in range(cols // 128):
                    wide[t] = block[k * 8 : k * 8 + 8, c * 128 : c * 128 + 128]
                    t += 1
    for i, eig in enumerate((a_eig, m_eig)):
        loads[2 + i].wait()
        for c in range(cols // 128):
            wide[t] = jnp.broadcast_to(eig[:, c * 128 : c * 128 + 128], (8, 128))
            t += 1
    loads[4].wait()

    def share(part, first, rows, base):
        for p in range(2 * rows // R):
            g = part[p * R : (p + 1) * R] * scale
            g = lax.dot_general(
                q[first + p], g, (((0,), (0,)), ((), ())), precision=HI, preferred_element_type=F32
            )
            for i in range(R // 8):
                half, local = divmod(p * R + i * 8, rows)
                for c in range(feats // 128):
                    at = (base + local) // 8 * (feats // 128) + c
                    halves[half, at] = g[i * 8 : i * 8 + 8, c * 128 : c * 128 + 128]

    loads[5].wait()
    loads[6].wait()
    part = lax.dot_general(a_h[...], a_in[...], (((1,), (0,)), ((), ())), preferred_element_type=F32)
    share(part, 0, HALF_A, 0)
    loads[7].wait()
    loads[8].wait()
    part = lax.dot_general(m_h[...], m_in[...], (((0,), (0,)), ((), ())), preferred_element_type=F32)
    share(part, CA // R, HALF_M, HALF_A)
    core = lax.axis_index("dp") % 2
    send[...] = halves[1 - core]
    keep[...] = halves[core]


def core_add_kernel(keep, both, out):
    core = lax.axis_index("dp") % 2
    out[...] = keep[...] + both[1 - core]


def rows_of(tiles, rows, first=0):
    cts = tiles.shape[0] // (HALF // 8)
    return jnp.concatenate(
        [
            jnp.concatenate([tiles[(first + r) * cts + c] for c in range(cts)], axis=1)
            for r in range(rows // 8)
        ]
    )


def sum_kernel(got, out):
    out[...] = (got[0] + got[1]) + (got[2] + got[3])


def add_kernel(one, two, out):
    out[...] = one[...] + two[...]


def rotate_kernel(pre, own, other, out, basis):
    feats, cols = basis.shape[0] // 2, basis.shape[1] // 2
    cts = cols // 128
    for side, source in enumerate((own, other)):
        for r in range(0, 2 * feats, 16):
            t = r // 8 * cts
            for c in range(cts):
                pair = jnp.concatenate([source[t + c], source[t + cts + c]])
                basis[r : r + 16, (side * cts + c) * 128 : (side * cts + c + 1) * 128] = pair.astype(BF16)
    rot_a = exact_dot(rows_of(pre, HALF_A), basis[:feats], 0)
    rot_m = exact_dot(rows_of(pre, HALF_M, HALF_A // 8), basis[feats:], 0)
    cts = 2 * cts
    for y in range(4):
        for rot, count, first, base in ((rot_a, Y_A // 8, y * Y_A, 0), (rot_m, Y_M // 8, y * Y_M, Y_A // 8)):
            for i in range(count):
                row = first + i * 8
                for c in range(cts):
                    out[y, (base + i) * cts + c] = rot[row : row + 8, c * 128 : c * 128 + 128]


def scale_kernel(one, two, own, other, eig, out):
    core = lax.axis_index("dp") % 2
    y = lax.axis_index("factor") // 4
    cts = one.shape[0] // ((Y_A + Y_M) // 8)
    eigs = own.shape[0] - cts
    lane = lax.broadcasted_iota(jnp.int32, (8, R), 1)
    sub = lax.broadcasted_iota(jnp.int32, (8, R), 0)
    quad = jnp.zeros((8, 128), F32)
    for rt in range((Y_A + Y_M) // 8):
        if rt < Y_A // 8:
            row, tail = core * HALF_A + y * Y_A + rt * 8, 0
        else:
            row, tail = CA + core * HALF_M + y * Y_M + (rt - Y_A // 8) * 8, cts // 2
        values = jnp.broadcast_to(eig[pl.ds(row // R, 1), :], (8, R))
        col = jnp.sum(jnp.where(lane == sub + row % R, values, 0.0), axis=1, keepdims=True)
        for c in range(cts):
            t = rt * cts + c
            rot = one[t] + two[t]
            source = own if c < cts // 2 else other
            scaled = rot / (col * source[eigs + tail + c % (cts // 2)] + damping)
            quad += scaled * rot
            for k in range(4):
                out[k, t] = scaled
    for k in range(4):
        out[k, out.shape[1] - 1] = quad


def back_kernel(got, basis, out):
    feats = basis.shape[0] // 2
    cts = basis.shape[1] // 128

    def gather(count, base):
        return jnp.concatenate(
            [
                jnp.concatenate([got[y, (base + i) * cts + c] for c in range(cts)], axis=1)
                for y in range(4)
                for i in range(count)
            ]
        )

    back_a = exact_dot(gather(Y_A // 8, 0), basis[:feats], 1)
    back_m = exact_dot(gather(Y_M // 8, Y_A // 8), basis[feats:], 1)
    fts = feats // 128
    per = HALF // 8 * fts // 16
    for back, count, base in ((back_a, HALF_A // 8, 0), (back_m, HALF_M // 8, HALF_A // 8)):
        for i in range(count):
            for c in range(fts):
                t = (base + i) * fts + c
                out[t // per, t % per] = back[i * 8 : i * 8 + 8, c * 128 : c * 128 + 128]
    last = got.shape[1] - 1
    quad = (got[0, last] + got[1, last]) + (got[2, last] + got[3, last])
    for k in range(16):
        out[k, per] = quad


def final_kernel(both, q, attn, mlp, result, stored):
    per = both.shape[2] - 1
    fts = attn.shape[1] // 128
    quad = jnp.sum(both[0, 0, per] + both[1, 0, per], keepdims=True)
    clip = jnp.minimum(1.0, jnp.sqrt(kl_limit / quad))
    stores = []
    for p in range(ROWS // R):
        rows = []
        for i in range(R // 8):
            row = p * R + i * 8
            if row < CA:
                half, local = divmod(row, HALF_A)
            else:
                half, local = divmod(row - CA, HALF_M)
                local += HALF_A
            ts = [local // 8 * fts + c for c in range(fts)]
            rows.append(jnp.concatenate([both[half, t // per, t % per] for t in ts], axis=1))
        b = jnp.concatenate(rows)
        b = clip * lax.dot_general(q[p], b, (((1,), (0,)), ((), ())), precision=HI, preferred_element_type=F32)
        result[p] = b
        target = attn.at[p * R : (p + 1) * R] if p * R < CA else mlp.at[p * R - CA : (p + 1) * R - CA]
        stores.append(pltpu.make_async_copy(result.at[p], target, stored.at[p]))
        stores[-1].start()
    for store in stores:
        store.wait()


def body(
    attn_in,
    mlp_in,
    attn_hgrad,
    mlp_hgrad,
    attn_basis,
    mlp_basis,
    attn_eig,
    mlp_eig,
    rank_basis,
    rank_eig,
):
    tokens, feats = attn_in.shape
    cols = attn_basis.shape[1]
    scale = 1.0 / (tokens * lax.axis_size("dp"))
    half_tiles = HALF // 8 * feats // 128
    y_tiles = HALF // 32 * 2 * cols // 128
    basis_tiles = 2 * (feats + 8) // 8 * cols // 128
    sources = (
        attn_basis,
        mlp_basis,
        attn_eig.reshape(1, -1),
        mlp_eig.reshape(1, -1),
        rank_basis,
        attn_hgrad.T,
        attn_in,
        mlp_hgrad,
        mlp_in,
    )
    send, keep, wide = pl.pallas_call(
        functools.partial(grad_kernel, scale),
        in_specs=[HBM] * len(sources),
        out_specs=[VMEM] * 3,
        out_shape=[shape(half_tiles, 8, 128), shape(half_tiles, 8, 128), shape(basis_tiles, 8, 128)],
        scratch_shapes=[pltpu.VMEM(s.shape, s.dtype) for s in sources]
        + [pltpu.VMEM((2, half_tiles, 8, 128), F32), pltpu.SemaphoreType.DMA((len(sources),))],
        compiler_params=LIMIT,
        name="grad",
    )(*far(*sources))
    other = lax.ppermute(wide, "dp", [(i, i ^ 1) for i in range(lax.axis_size("dp"))])
    both = lax.all_gather(send, "dp", axis_index_groups=CORE_PAIRS)
    part = pl.pallas_call(
        core_add_kernel,
        in_specs=[VMEM] * 2,
        out_specs=VMEM,
        out_shape=shape(half_tiles, 8, 128),
        compiler_params=LIMIT,
        name="core_add",
    )(*near(keep, both))
    part, other = lax.optimization_barrier((part, other))
    shard = jnp.sum(exchange(part.reshape(16, -1, 8, 128), "dp", CHIPS), axis=0)
    pre = exchange(copies(shard, 16), "dp", CHIPS).reshape(-1, 8, 128)

    block, basis = pl.pallas_call(
        rotate_kernel,
        in_specs=[VMEM] * 3,
        out_specs=[VMEM] * 2,
        out_shape=[shape(4, y_tiles, 8, 128), shape(2 * feats, 2 * cols, dtype=BF16)],
        compiler_params=LIMIT,
        name="rotate",
    )(*near(pre, wide, other))
    block = pl.pallas_call(
        sum_kernel,
        in_specs=[VMEM],
        out_specs=VMEM,
        out_shape=shape(y_tiles, 8, 128),
        compiler_params=LIMIT,
        name="y_sum",
    )(*near(exchange(block, "factor", Y_GROUPS)))
    block = pl.pallas_call(
        add_kernel,
        in_specs=[VMEM] * 2,
        out_specs=VMEM,
        out_shape=shape(y_tiles, 8, 128),
        compiler_params=LIMIT,
        name="z_add",
    )(*near(block, lax.ppermute(block, "factor", Z_PAIRS)))
    across = lax.ppermute(block, "factor", Z_CROSS)
    scaled = pl.pallas_call(
        scale_kernel,
        in_specs=[VMEM] * 5,
        out_specs=VMEM,
        out_shape=shape(4, y_tiles + 1, 8, 128),
        compiler_params=LIMIT,
        name="scale",
    )(*near(block, across, wide, other, rank_eig))
    scaled = exchange(scaled, "factor", Y_GROUPS)
    back = pl.pallas_call(
        back_kernel,
        in_specs=[VMEM] * 2,
        out_specs=VMEM,
        out_shape=shape(16, half_tiles // 16 + 1, 8, 128),
        compiler_params=LIMIT, name="back",
    )(*near(scaled, basis))
    summed = jnp.sum(exchange(back, "dp", CHIPS), axis=0)
    back = exchange(copies(summed, 16), "dp", CHIPS)
    both = lax.all_gather(back, "dp", axis_index_groups=CORE_PAIRS)
    return tuple(
        pl.pallas_call(
            final_kernel,
            in_specs=[VMEM] * 2,
            out_specs=[HBM] * 2,
            scratch_shapes=[pltpu.VMEM((ROWS // R, R, feats), F32), pltpu.SemaphoreType.DMA((ROWS // R,))],
            compiler_params=LIMIT,
            out_shape=[jax.ShapeDtypeStruct((CA, feats), F32), jax.ShapeDtypeStruct((CM, feats), F32)],
            name="final",
        )(*near(both, rank_basis))
    )


def solution(mesh):
    in_specs = (
        P("dp", "factor"),
        P("dp", "factor"),
        P("dp", None),
        P("dp", None),
        P("factor", "dp"),
        P("factor", "dp"),
        P("dp"),
        P("dp"),
        P(),
        P(),
    )
    out_specs = (P(None, "factor"), P(None, "factor"))


    return jax.shard_map(body, mesh=mesh, in_specs=in_specs, out_specs=out_specs, check_vma=False)
```

```python
import functools

import jax
import jax.numpy as jnp
from jax import lax
from jax.experimental import pallas as pl
from jax.experimental.pallas import tpu as pltpu
from jax.sharding import PartitionSpec as P

damping = 0.001
kl_limit = 8000.0
F32, BF16 = jnp.float32, jnp.bfloat16

CORE_PAIRS = [[x * 8 + z * 2 + c for c in range(2)] for x in range(4) for z in range(4)]
CHIPS = [[x * 8 + z * 2 + c for x in range(4) for z in range(4)] for c in range(2)]
Y_GROUPS = [[y * 4 + z for y in range(4)] for z in range(4)]
Z_PAIRS = [(y * 4 + z, y * 4 + (z ^ 1)) for y in range(4) for z in range(4)]
Z_CROSS = [(y * 4 + z, y * 4 + 3 - z) for y in range(4) for z in range(4)]

CA, CM, R = 192, 128, 64
ROWS, HALF_A, HALF_M = CA + CM, CA // 2, CM // 2
HALF = HALF_A + HALF_M
Y_A, Y_M = HALF_A // 4, HALF_M // 4


def exchange(x, axis, groups):
    return lax.all_to_all(x, axis, 0, 0, axis_index_groups=groups, tiled=True)


def copies(x, count):
    return jnp.broadcast_to(x[None], (count,) + x.shape)


def shape(*dims, dtype=F32):
    return pltpu.VMEM(dims, dtype)


def far(*arrays):
    return [pltpu.with_memory_space_constraint(a, pltpu.HBM) for a in arrays]


def near(*arrays):
    return [pltpu.with_memory_space_constraint(a, pltpu.VMEM) for a in arrays]


LIMIT = pltpu.CompilerParams(vmem_limit_bytes=12 * 2**20)
VMEM = pl.BlockSpec(memory_space=pltpu.VMEM)
HBM = pl.BlockSpec(memory_space=pltpu.HBM)


def pieces(x):
    a = x.astype(BF16)
    r = x - a.astype(F32)
    b = r.astype(BF16)
    return a, b, (r - b.astype(F32)).astype(BF16)


def exact_dot(x, basis, contract):
    n = x.shape[0]
    stacked = jnp.concatenate(pieces(x), axis=0)
    out = lax.dot_general(stacked, basis, (((1,), (contract,)), ((), ())), preferred_element_type=F32)
    return (out[2 * n :] + out[n : 2 * n]) + out[:n]


def rank_dot(blocks, x):
    qa, qb, qc = pieces(blocks)
    a, b, c = pieces(x)
    left = jnp.concatenate([qc, qa, qb, qb, qa, qa], axis=1)
    right = jnp.concatenate([a, c, b, a, b, a], axis=0)
    return lax.dot_general(left, right, (((1,), (0,)), ((), ())), preferred_element_type=F32)


def grad_kernel(scale, *refs):
    sources, (send, keep, wide), landed = refs[:9], refs[9:12], refs[12:21]
    halves, arrived = refs[21:]
    loads = [pltpu.make_async_copy(s, d, arrived.at[i]) for i, (s, d) in enumerate(zip(sources, landed))]
    for load in loads:
        load.start()
    a_b, m_b, a_eig, m_eig, q, a_h, a_in, m_h, m_in = landed
    feats, cols = a_b.shape
    t = 0
    for i, basis in enumerate((a_b, m_b)):
        loads[i].wait()
        for r in range(0, feats, 16):
            block = basis[r : r + 16].astype(F32)
            for k in range(2):
                for c in range(cols // 128):
                    wide[t] = block[k * 8 : k * 8 + 8, c * 128 : c * 128 + 128]
                    t += 1
    for i, eig in enumerate((a_eig, m_eig)):
        loads[2 + i].wait()
        for c in range(cols // 128):
            wide[t] = jnp.broadcast_to(eig[:, c * 128 : c * 128 + 128], (8, 128))
            t += 1
    loads[4].wait()

    def share(part, first, rows, base):
        for p in range(2 * rows // R):
            g = rank_dot(q[first + p].T, part[p * R : (p + 1) * R] * scale)
            for i in range(R // 8):
                half, local = divmod(p * R + i * 8, rows)
                for c in range(feats // 128):
                    at = (base + local) // 8 * (feats // 128) + c
                    halves[half, at] = g[i * 8 : i * 8 + 8, c * 128 : c * 128 + 128]

    loads[5].wait()
    loads[6].wait()
    part = lax.dot_general(a_h[...], a_in[...], (((1,), (0,)), ((), ())), preferred_element_type=F32)
    share(part, 0, HALF_A, 0)
    loads[7].wait()
    loads[8].wait()
    part = lax.dot_general(m_h[...], m_in[...], (((0,), (0,)), ((), ())), preferred_element_type=F32)
    share(part, CA // R, HALF_M, HALF_A)
    core = lax.axis_index("dp") % 2
    send[...] = halves[1 - core]
    keep[...] = halves[core]


def core_add_kernel(keep, both, out):
    core = lax.axis_index("dp") % 2
    out[...] = keep[...] + both[1 - core]


def rows_of(tiles, rows, first=0):
    cts = tiles.shape[0] // (HALF // 8)
    return jnp.concatenate(
        [
            jnp.concatenate([tiles[(first + r) * cts + c] for c in range(cts)], axis=1)
            for r in range(rows // 8)
        ]
    )


def sum_kernel(got, out):
    out[...] = (got[0] + got[1]) + (got[2] + got[3])


def add_kernel(one, two, out):
    out[...] = one[...] + two[...]


def rotate_kernel(pre, own, other, out, basis):
    feats, cols = basis.shape[0] // 2, basis.shape[1] // 2
    cts = cols // 128
    for side, source in enumerate((own, other)):
        for r in range(0, 2 * feats, 16):
            t = r // 8 * cts
            for c in range(cts):
                pair = jnp.concatenate([source[t + c], source[t + cts + c]])
                basis[r : r + 16, (side * cts + c) * 128 : (side * cts + c + 1) * 128] = pair.astype(BF16)
    rot_a = exact_dot(rows_of(pre, HALF_A), basis[:feats], 0)
    rot_m = exact_dot(rows_of(pre, HALF_M, HALF_A // 8), basis[feats:], 0)
    cts = 2 * cts
    for y in range(4):
        for rot, count, first, base in ((rot_a, Y_A // 8, y * Y_A, 0), (rot_m, Y_M // 8, y * Y_M, Y_A // 8)):
            for i in range(count):
                row = first + i * 8
                for c in range(cts):
                    out[y, (base + i) * cts + c] = rot[row : row + 8, c * 128 : c * 128 + 128]


def scale_kernel(one, two, own, other, eig, out):
    core = lax.axis_index("dp") % 2
    y = lax.axis_index("factor") // 4
    cts = one.shape[0] // ((Y_A + Y_M) // 8)
    eigs = own.shape[0] - cts
    lane = lax.broadcasted_iota(jnp.int32, (8, R), 1)
    sub = lax.broadcasted_iota(jnp.int32, (8, R), 0)
    quad = jnp.zeros((8, 128), F32)
    for rt in range((Y_A + Y_M) // 8):
        if rt < Y_A // 8:
            row, tail = core * HALF_A + y * Y_A + rt * 8, 0
        else:
            row, tail = CA + core * HALF_M + y * Y_M + (rt - Y_A // 8) * 8, cts // 2
        values = jnp.broadcast_to(eig[pl.ds(row // R, 1), :], (8, R))
        col = jnp.sum(jnp.where(lane == sub + row % R, values, 0.0), axis=1, keepdims=True)
        for c in range(cts):
            t = rt * cts + c
            rot = one[t] + two[t]
            source = own if c < cts // 2 else other
            scaled = rot / (col * source[eigs + tail + c % (cts // 2)] + damping)
            quad += scaled * rot
            for k in range(4):
                out[k, t] = scaled
    for k in range(4):
        out[k, out.shape[1] - 1] = quad


def back_kernel(got, basis, out):
    feats = basis.shape[0] // 2
    cts = basis.shape[1] // 128

    def gather(count, base):
        return jnp.concatenate(
            [
                jnp.concatenate([got[y, (base + i) * cts + c] for c in range(cts)], axis=1)
                for y in range(4)
                for i in range(count)
            ]
        )

    back_a = exact_dot(gather(Y_A // 8, 0), basis[:feats], 1)
    back_m = exact_dot(gather(Y_M // 8, Y_A // 8), basis[feats:], 1)
    fts = feats // 128
    per = HALF // 8 * fts // 16
    for back, count, base in ((back_a, HALF_A // 8, 0), (back_m, HALF_M // 8, HALF_A // 8)):
        for i in range(count):
            for c in range(fts):
                t = (base + i) * fts + c
                out[t // per, t % per] = back[i * 8 : i * 8 + 8, c * 128 : c * 128 + 128]
    last = got.shape[1] - 1
    quad = (got[0, last] + got[1, last]) + (got[2, last] + got[3, last])
    for k in range(16):
        out[k, per] = quad


def final_kernel(both, q, attn, mlp, result, stored):
    per = both.shape[2] - 1
    fts = attn.shape[1] // 128
    quad = jnp.sum(both[0, 0, per] + both[1, 0, per], keepdims=True)
    clip = jnp.minimum(1.0, jnp.sqrt(kl_limit / quad))
    stores = []
    for p in range(ROWS // R):
        rows = []
        for i in range(R // 8):
            row = p * R + i * 8
            if row < CA:
                half, local = divmod(row, HALF_A)
            else:
                half, local = divmod(row - CA, HALF_M)
                local += HALF_A
            ts = [local // 8 * fts + c for c in range(fts)]
            rows.append(jnp.concatenate([both[half, t // per, t % per] for t in ts], axis=1))
        b = jnp.concatenate(rows)
        b = clip * rank_dot(q[p], b)
        result[p] = b
        target = attn.at[p * R : (p + 1) * R] if p * R < CA else mlp.at[p * R - CA : (p + 1) * R - CA]
        stores.append(pltpu.make_async_copy(result.at[p], target, stored.at[p]))
        stores[-1].start()
    for store in stores:
        store.wait()


def body(
    attn_in,
    mlp_in,
    attn_hgrad,
    mlp_hgrad,
    attn_basis,
    mlp_basis,
    attn_eig,
    mlp_eig,
    rank_basis,
    rank_eig,
):
    tokens, feats = attn_in.shape
    cols = attn_basis.shape[1]
    scale = 1.0 / (tokens * lax.axis_size("dp"))
    half_tiles = HALF // 8 * feats // 128
    y_tiles = HALF // 32 * 2 * cols // 128
    basis_tiles = 2 * (feats + 8) // 8 * cols // 128
    sources = (
        attn_basis,
        mlp_basis,
        attn_eig.reshape(1, -1),
        mlp_eig.reshape(1, -1),
        rank_basis,
        attn_hgrad.T,
        attn_in,
        mlp_hgrad,
        mlp_in,
    )
    send, keep, wide = pl.pallas_call(
        functools.partial(grad_kernel, scale),
        in_specs=[HBM] * len(sources),
        out_specs=[VMEM] * 3,
        out_shape=[shape(half_tiles, 8, 128), shape(half_tiles, 8, 128), shape(basis_tiles, 8, 128)],
        scratch_shapes=[pltpu.VMEM(s.shape, s.dtype) for s in sources]
        + [pltpu.VMEM((2, half_tiles, 8, 128), F32), pltpu.SemaphoreType.DMA((len(sources),))],
        compiler_params=LIMIT,
        name="grad",
    )(*far(*sources))
    other = lax.ppermute(wide, "dp", [(i, i ^ 1) for i in range(lax.axis_size("dp"))])
    both = lax.all_gather(send, "dp", axis_index_groups=CORE_PAIRS)
    part = pl.pallas_call(
        core_add_kernel,
        in_specs=[VMEM] * 2,
        out_specs=VMEM,
        out_shape=shape(half_tiles, 8, 128),
        compiler_params=LIMIT,
        name="core_add",
    )(*near(keep, both))
    shard, other = lax.optimization_barrier((exchange(part.reshape(16, -1, 8, 128), "dp", CHIPS), other))
    shard = jnp.sum(shard, axis=0)
    pre = exchange(copies(shard, 16), "dp", CHIPS).reshape(-1, 8, 128)

    block, basis = pl.pallas_call(
        rotate_kernel,
        in_specs=[VMEM] * 3,
        out_specs=[VMEM] * 2,
        out_shape=[shape(4, y_tiles, 8, 128), shape(2 * feats, 2 * cols, dtype=BF16)],
        compiler_params=LIMIT,
        name="rotate",
    )(*near(pre, wide, other))
    block = pl.pallas_call(
        sum_kernel,
        in_specs=[VMEM],
        out_specs=VMEM,
        out_shape=shape(y_tiles, 8, 128),
        compiler_params=LIMIT,
        name="y_sum",
    )(*near(exchange(block, "factor", Y_GROUPS)))
    block = pl.pallas_call(
        add_kernel,
        in_specs=[VMEM] * 2,
        out_specs=VMEM,
        out_shape=shape(y_tiles, 8, 128),
        compiler_params=LIMIT,
        name="z_add",
    )(*near(block, lax.ppermute(block, "factor", Z_PAIRS)))
    across = lax.ppermute(block, "factor", Z_CROSS)
    scaled = pl.pallas_call(
        scale_kernel,
        in_specs=[VMEM] * 5,
        out_specs=VMEM,
        out_shape=shape(4, y_tiles + 1, 8, 128),
        compiler_params=LIMIT,
        name="scale",
    )(*near(block, across, wide, other, rank_eig))
    scaled = exchange(scaled, "factor", Y_GROUPS)
    back = pl.pallas_call(
        back_kernel,
        in_specs=[VMEM] * 2,
        out_specs=VMEM,
        out_shape=shape(16, half_tiles // 16 + 1, 8, 128),
        compiler_params=LIMIT, name="back",
    )(*near(scaled, basis))
    summed = jnp.sum(exchange(back, "dp", CHIPS), axis=0)
    back = exchange(copies(summed, 16), "dp", CHIPS)
    both = lax.all_gather(back, "dp", axis_index_groups=CORE_PAIRS)
    return tuple(
        pl.pallas_call(
            final_kernel,
            in_specs=[VMEM] * 2,
            out_specs=[HBM] * 2,
            scratch_shapes=[pltpu.VMEM((ROWS // R, R, feats), F32), pltpu.SemaphoreType.DMA((ROWS // R,))],
            compiler_params=LIMIT,
            out_shape=[jax.ShapeDtypeStruct((CA, feats), F32), jax.ShapeDtypeStruct((CM, feats), F32)],
            name="final",
        )(*near(both, rank_basis))
    )


def solution(mesh):
    in_specs = (
        P("dp", "factor"),
        P("dp", "factor"),
        P("dp", None),
        P("dp", None),
        P("factor", "dp"),
        P("factor", "dp"),
        P("dp"),
        P("dp"),
        P(),
        P(),
    )
    out_specs = (P(None, "factor"), P(None, "factor"))

    return jax.shard_map(body, mesh=mesh, in_specs=in_specs, out_specs=out_specs, check_vma=False)
```

```python
import functools

import jax
import jax.numpy as jnp
from jax import lax
from jax.experimental import pallas as pl
from jax.experimental.pallas import tpu as pltpu
from jax.sharding import PartitionSpec as P

damping = 0.001
kl_limit = 8000.0
F32, BF16 = jnp.float32, jnp.bfloat16

CORE_PAIRS = [[x * 8 + z * 2 + c for c in range(2)] for x in range(4) for z in range(4)]
CHIPS = [[x * 8 + z * 2 + c for x in range(4) for z in range(4)] for c in range(2)]
Y_GROUPS = [[y * 4 + z for y in range(4)] for z in range(4)]
Z_PAIRS = [(y * 4 + z, y * 4 + (z ^ 1)) for y in range(4) for z in range(4)]
Z_CROSS = [(y * 4 + z, y * 4 + 3 - z) for y in range(4) for z in range(4)]

CA, CM, R = 192, 128, 64
ROWS, HALF_A, HALF_M = CA + CM, CA // 2, CM // 2
HALF = HALF_A + HALF_M
Y_A, Y_M = HALF_A // 4, HALF_M // 4


def exchange(x, axis, groups):
    return lax.all_to_all(x, axis, 0, 0, axis_index_groups=groups, tiled=True)


def copies(x, count):
    return jnp.broadcast_to(x[None], (count,) + x.shape)


def shape(*dims, dtype=F32):
    return pltpu.VMEM(dims, dtype)


def far(*arrays):
    return [pltpu.with_memory_space_constraint(a, pltpu.HBM) for a in arrays]


def near(*arrays):
    return [pltpu.with_memory_space_constraint(a, pltpu.VMEM) for a in arrays]


LIMIT = pltpu.CompilerParams(vmem_limit_bytes=12 * 2**20)
VMEM = pl.BlockSpec(memory_space=pltpu.VMEM)
HBM = pl.BlockSpec(memory_space=pltpu.HBM)


def pieces(x):
    a = x.astype(BF16)
    r = x - a.astype(F32)
    b = r.astype(BF16)
    return a, b, (r - b.astype(F32)).astype(BF16)


def exact_dot(x, basis, contract):
    n = x.shape[0]
    stacked = jnp.concatenate(pieces(x), axis=0)
    out = lax.dot_general(stacked, basis, (((1,), (contract,)), ((), ())), preferred_element_type=F32)
    return (out[2 * n :] + out[n : 2 * n]) + out[:n]


def rank_dot(blocks, x):
    qa, qb, qc = pieces(blocks)
    a, b, c = pieces(x)
    left = jnp.concatenate([qc, qa, qb, qb, qa, qa], axis=1)
    right = jnp.concatenate([a, c, b, a, b, a], axis=0)
    return lax.dot_general(left, right, (((1,), (0,)), ((), ())), preferred_element_type=F32)


def widen_kernel(a_b, m_b, a_eig, m_eig, wide):
    t = 0
    feats, cols = a_b.shape
    for basis in (a_b, m_b):
        for r in range(0, feats, 16):
            block = basis[r : r + 16].astype(F32)
            for k in range(2):
                for c in range(cols // 128):
                    wide[t] = block[k * 8 : k * 8 + 8, c * 128 : c * 128 + 128]
                    t += 1
    for eig in (a_eig, m_eig):
        for c in range(cols // 128):
            wide[t] = jnp.broadcast_to(eig[:, c * 128 : c * 128 + 128], (8, 128))
            t += 1


def join_kernel(own, other, basis):
    rows, cols = basis.shape
    cts = cols // 256
    for side, source in enumerate((own, other)):
        for r in range(0, rows, 16):
            t = r // 8 * cts
            for c in range(cts):
                pair = jnp.concatenate([source[t + c], source[t + cts + c]])
                basis[r : r + 16, (side * cts + c) * 128 : (side * cts + c + 1) * 128] = pair.astype(BF16)


def grad_kernel(scale, *refs):
    sources, (send, keep), landed = refs[:5], refs[5:7], refs[7:12]
    halves, arrived = refs[12:]
    loads = [pltpu.make_async_copy(s, d, arrived.at[i]) for i, (s, d) in enumerate(zip(sources, landed))]
    for load in loads:
        load.start()
    q, a_h, a_in, m_h, m_in = landed
    feats = a_in.shape[1]
    loads[0].wait()

    def share(part, first, rows, base):
        for p in range(2 * rows // R):
            g = rank_dot(q[first + p].T, part[p * R : (p + 1) * R] * scale)
            for i in range(R // 8):
                half, local = divmod(p * R + i * 8, rows)
                for c in range(feats // 128):
                    at = (base + local) // 8 * (feats // 128) + c
                    halves[half, at] = g[i * 8 : i * 8 + 8, c * 128 : c * 128 + 128]

    loads[1].wait()
    loads[2].wait()
    part = lax.dot_general(a_h[...], a_in[...], (((1,), (0,)), ((), ())), preferred_element_type=F32)
    share(part, 0, HALF_A, 0)
    loads[3].wait()
    loads[4].wait()
    part = lax.dot_general(m_h[...], m_in[...], (((0,), (0,)), ((), ())), preferred_element_type=F32)
    share(part, CA // R, HALF_M, HALF_A)
    core = lax.axis_index("dp") % 2
    send[...] = halves[1 - core]
    keep[...] = halves[core]


def core_add_kernel(keep, both, out):
    core = lax.axis_index("dp") % 2
    out[...] = keep[...] + both[1 - core]


def rows_of(tiles, rows, first=0):
    cts = tiles.shape[0] // (HALF // 8)
    return jnp.concatenate(
        [
            jnp.concatenate([tiles[(first + r) * cts + c] for c in range(cts)], axis=1)
            for r in range(rows // 8)
        ]
    )


def sum_kernel(got, out):
    out[...] = (got[0] + got[1]) + (got[2] + got[3])


def add_kernel(one, two, out):
    out[...] = one[...] + two[...]


def rotate_kernel(pre, basis, out):
    feats, cts = basis.shape[0] // 2, basis.shape[1] // 128
    rot_a = exact_dot(rows_of(pre, HALF_A), basis[:feats], 0)
    rot_m = exact_dot(rows_of(pre, HALF_M, HALF_A // 8), basis[feats:], 0)
    for y in range(4):
        for rot, count, first, base in ((rot_a, Y_A // 8, y * Y_A, 0), (rot_m, Y_M // 8, y * Y_M, Y_A // 8)):
            for i in range(count):
                row = first + i * 8
                for c in range(cts):
                    out[y, (base + i) * cts + c] = rot[row : row + 8, c * 128 : c * 128 + 128]


def scale_kernel(one, two, own, other, eig, out):
    core = lax.axis_index("dp") % 2
    y = lax.axis_index("factor") // 4
    cts = one.shape[0] // ((Y_A + Y_M) // 8)
    eigs = own.shape[0] - cts
    lane = lax.broadcasted_iota(jnp.int32, (8, R), 1)
    sub = lax.broadcasted_iota(jnp.int32, (8, R), 0)
    quad = jnp.zeros((8, 128), F32)
    for rt in range((Y_A + Y_M) // 8):
        if rt < Y_A // 8:
            row, tail = core * HALF_A + y * Y_A + rt * 8, 0
        else:
            row, tail = CA + core * HALF_M + y * Y_M + (rt - Y_A // 8) * 8, cts // 2
        values = jnp.broadcast_to(eig[pl.ds(row // R, 1), :], (8, R))
        col = jnp.sum(jnp.where(lane == sub + row % R, values, 0.0), axis=1, keepdims=True)
        for c in range(cts):
            t = rt * cts + c
            rot = one[t] + two[t]
            source = own if c < cts // 2 else other
            scaled = rot / (col * source[eigs + tail + c % (cts // 2)] + damping)
            quad += scaled * rot
            for k in range(4):
                out[k, t] = scaled
    for k in range(4):
        out[k, out.shape[1] - 1] = quad


def back_kernel(got, basis, out):
    feats = basis.shape[0] // 2
    cts = basis.shape[1] // 128

    def gather(count, base):
        return jnp.concatenate(
            [
                jnp.concatenate([got[y, (base + i) * cts + c] for c in range(cts)], axis=1)
                for y in range(4)
                for i in range(count)
            ]
        )

    back_a = exact_dot(gather(Y_A // 8, 0), basis[:feats], 1)
    back_m = exact_dot(gather(Y_M // 8, Y_A // 8), basis[feats:], 1)
    fts = feats // 128
    per = HALF // 8 * fts // 16
    for back, count, base in ((back_a, HALF_A // 8, 0), (back_m, HALF_M // 8, HALF_A // 8)):
        for i in range(count):
            for c in range(fts):
                t = (base + i) * fts + c
                out[t // per, t % per] = back[i * 8 : i * 8 + 8, c * 128 : c * 128 + 128]
    last = got.shape[1] - 1
    quad = (got[0, last] + got[1, last]) + (got[2, last] + got[3, last])
    for k in range(16):
        out[k, per] = quad


def final_kernel(both, q, attn, mlp, result, stored):
    per = both.shape[2] - 1
    fts = attn.shape[1] // 128
    quad = jnp.sum(both[0, 0, per] + both[1, 0, per], keepdims=True)
    clip = jnp.minimum(1.0, jnp.sqrt(kl_limit / quad))
    stores = []
    for p in range(ROWS // R):
        rows = []
        for i in range(R // 8):
            row = p * R + i * 8
            if row < CA:
                half, local = divmod(row, HALF_A)
            else:
                half, local = divmod(row - CA, HALF_M)
                local += HALF_A
            ts = [local // 8 * fts + c for c in range(fts)]
            rows.append(jnp.concatenate([both[half, t // per, t % per] for t in ts], axis=1))
        b = jnp.concatenate(rows)
        b = clip * rank_dot(q[p], b)
        result[p] = b
        target = attn.at[p * R : (p + 1) * R] if p * R < CA else mlp.at[p * R - CA : (p + 1) * R - CA]
        stores.append(pltpu.make_async_copy(result.at[p], target, stored.at[p]))
        stores[-1].start()
    for store in stores:
        store.wait()


def body(
    attn_in,
    mlp_in,
    attn_hgrad,
    mlp_hgrad,
    attn_basis,
    mlp_basis,
    attn_eig,
    mlp_eig,
    rank_basis,
    rank_eig,
):
    tokens, feats = attn_in.shape
    cols = attn_basis.shape[1]
    scale = 1.0 / (tokens * lax.axis_size("dp"))
    half_tiles = HALF // 8 * feats // 128
    y_tiles = HALF // 32 * 2 * cols // 128
    basis_tiles = 2 * (feats + 8) // 8 * cols // 128
    sources = (rank_basis, attn_hgrad.T, attn_in, mlp_hgrad, mlp_in)
    send, keep = pl.pallas_call(
        functools.partial(grad_kernel, scale),
        in_specs=[HBM] * len(sources),
        out_specs=[VMEM] * 2,
        out_shape=[shape(half_tiles, 8, 128)] * 2,
        scratch_shapes=[pltpu.VMEM(s.shape, s.dtype) for s in sources]
        + [pltpu.VMEM((2, half_tiles, 8, 128), F32), pltpu.SemaphoreType.DMA((len(sources),))],
        compiler_params=LIMIT,
        name="grad",
    )(*far(*sources))
    both = lax.all_gather(send, "dp", axis_index_groups=CORE_PAIRS)
    part = pl.pallas_call(
        core_add_kernel,
        in_specs=[VMEM] * 2,
        out_specs=VMEM,
        out_shape=shape(half_tiles, 8, 128),
        compiler_params=LIMIT,
        name="core_add",
    )(*near(keep, both))

    part, attn_basis, mlp_basis = lax.optimization_barrier((part, attn_basis, mlp_basis))
    wide = pl.pallas_call(
        widen_kernel,
        in_specs=[VMEM] * 4,
        out_specs=VMEM,
        out_shape=shape(basis_tiles, 8, 128),
        compiler_params=LIMIT,
        name="widen",
    )(*near(attn_basis, mlp_basis, attn_eig.reshape(1, -1), mlp_eig.reshape(1, -1)))
    other = lax.ppermute(wide, "dp", [(i, i ^ 1) for i in range(lax.axis_size("dp"))])
    basis = pl.pallas_call(
        join_kernel,
        in_specs=[VMEM] * 2,
        out_specs=VMEM,
        out_shape=shape(2 * feats, 2 * cols, dtype=BF16),
        compiler_params=LIMIT,
        name="join",
    )(*near(wide, other))
    shard, basis = lax.optimization_barrier((exchange(part.reshape(16, -1, 8, 128), "dp", CHIPS), basis))
    shard = jnp.sum(shard, axis=0)
    pre = exchange(copies(shard, 16), "dp", CHIPS).reshape(-1, 8, 128)

    block = pl.pallas_call(
        rotate_kernel,
        in_specs=[VMEM] * 2,
        out_specs=VMEM,
        out_shape=shape(4, y_tiles, 8, 128),
        compiler_params=LIMIT,
        name="rotate",
    )(*near(pre, basis))
    block = pl.pallas_call(
        sum_kernel,
        in_specs=[VMEM],
        out_specs=VMEM,
        out_shape=shape(y_tiles, 8, 128),
        compiler_params=LIMIT,
        name="y_sum",
    )(*near(exchange(block, "factor", Y_GROUPS)))
    block = pl.pallas_call(
        add_kernel,
        in_specs=[VMEM] * 2,
        out_specs=VMEM,
        out_shape=shape(y_tiles, 8, 128),
        compiler_params=LIMIT,
        name="z_add",
    )(*near(block, lax.ppermute(block, "factor", Z_PAIRS)))
    across = lax.ppermute(block, "factor", Z_CROSS)
    scaled = pl.pallas_call(
        scale_kernel,
        in_specs=[VMEM] * 5,
        out_specs=VMEM,
        out_shape=shape(4, y_tiles + 1, 8, 128),
        compiler_params=LIMIT,
        name="scale",
    )(*near(block, across, wide, other, rank_eig))
    scaled = exchange(scaled, "factor", Y_GROUPS)
    back = pl.pallas_call(
        back_kernel,
        in_specs=[VMEM] * 2,
        out_specs=VMEM,
        out_shape=shape(16, half_tiles // 16 + 1, 8, 128),
        compiler_params=LIMIT, name="back",
    )(*near(scaled, basis))
    summed = jnp.sum(exchange(back, "dp", CHIPS), axis=0)
    back = exchange(copies(summed, 16), "dp", CHIPS)
    both = lax.all_gather(back, "dp", axis_index_groups=CORE_PAIRS)
    return tuple(
        pl.pallas_call(
            final_kernel,
            in_specs=[VMEM] * 2,
            out_specs=[HBM] * 2,
            scratch_shapes=[pltpu.VMEM((ROWS // R, R, feats), F32), pltpu.SemaphoreType.DMA((ROWS // R,))],
            compiler_params=LIMIT,
            out_shape=[jax.ShapeDtypeStruct((CA, feats), F32), jax.ShapeDtypeStruct((CM, feats), F32)],
            name="final",
        )(*near(both, rank_basis))
    )


def solution(mesh):
    in_specs = (
        P("dp", "factor"),
        P("dp", "factor"),
        P("dp", None),
        P("dp", None),
        P("factor", "dp"),
        P("factor", "dp"),
        P("dp"),
        P("dp"),
        P(),
        P(),
    )
    out_specs = (P(None, "factor"), P(None, "factor"))

    return jax.shard_map(body, mesh=mesh, in_specs=in_specs, out_specs=out_specs, check_vma=False)
```

```python
import functools

import jax
import jax.numpy as jnp
from jax import lax
from jax.experimental import pallas as pl
from jax.experimental.pallas import tpu as pltpu
from jax.sharding import PartitionSpec as P

damping = 0.001
kl_limit = 8000.0
F32, BF16 = jnp.float32, jnp.bfloat16

CORE_PAIRS = [[x * 8 + z * 2 + c for c in range(2)] for x in range(4) for z in range(4)]
CHIPS = [[x * 8 + z * 2 + c for x in range(4) for z in range(4)] for c in range(2)]
Y_GROUPS = [[y * 4 + z for y in range(4)] for z in range(4)]
Z_PAIRS = [(y * 4 + z, y * 4 + (z ^ 1)) for y in range(4) for z in range(4)]
Z_CROSS = [(y * 4 + z, y * 4 + 3 - z) for y in range(4) for z in range(4)]

CA, CM, R = 192, 128, 64
ROWS, HALF_A, HALF_M = CA + CM, CA // 2, CM // 2
HALF = HALF_A + HALF_M
Y_A, Y_M = HALF_A // 4, HALF_M // 4


def exchange(x, axis, groups):
    return lax.all_to_all(x, axis, 0, 0, axis_index_groups=groups, tiled=True)


def copies(x, count):
    return jnp.broadcast_to(x[None], (count,) + x.shape)


def shape(*dims, dtype=F32):
    return pltpu.VMEM(dims, dtype)


def far(*arrays):
    return [pltpu.with_memory_space_constraint(a, pltpu.HBM) for a in arrays]


def near(*arrays):
    return [pltpu.with_memory_space_constraint(a, pltpu.VMEM) for a in arrays]


LIMIT = pltpu.CompilerParams(vmem_limit_bytes=12 * 2**20)
VMEM = pl.BlockSpec(memory_space=pltpu.VMEM)
HBM = pl.BlockSpec(memory_space=pltpu.HBM)


def pieces(x):
    a = x.astype(BF16)
    r = x - a.astype(F32)
    b = r.astype(BF16)
    return a, b, (r - b.astype(F32)).astype(BF16)


def exact_dot(x, basis, contract):
    n = x.shape[0]
    stacked = jnp.concatenate(pieces(x), axis=0)
    out = lax.dot_general(stacked, basis, (((1,), (contract,)), ((), ())), preferred_element_type=F32)
    return (out[2 * n :] + out[n : 2 * n]) + out[:n]


def rank_dot(blocks, x):
    qa, qb, _ = pieces(blocks)
    a, b, _ = pieces(x)
    left = jnp.concatenate([qb, qa, qb, qa], axis=1)
    right = jnp.concatenate([b, b, a, a], axis=0)
    return lax.dot_general(left, right, (((1,), (0,)), ((), ())), preferred_element_type=F32)


def widen_kernel(a_b, m_b, a_eig, m_eig, wide):
    t = 0
    feats, cols = a_b.shape
    for basis in (a_b, m_b):
        for r in range(0, feats, 16):
            block = basis[r : r + 16].astype(F32)
            for k in range(2):
                for c in range(cols // 128):
                    wide[t] = block[k * 8 : k * 8 + 8, c * 128 : c * 128 + 128]
                    t += 1
    for eig in (a_eig, m_eig):
        for c in range(cols // 128):
            wide[t] = jnp.broadcast_to(eig[:, c * 128 : c * 128 + 128], (8, 128))
            t += 1


def join_kernel(own, other, basis):
    rows, cols = basis.shape
    cts = cols // 256
    for side, source in enumerate((own, other)):
        for r in range(0, rows, 16):
            t = r // 8 * cts
            for c in range(cts):
                pair = jnp.concatenate([source[t + c], source[t + cts + c]])
                basis[r : r + 16, (side * cts + c) * 128 : (side * cts + c + 1) * 128] = pair.astype(BF16)


def grad_kernel(scale, *refs):
    sources, (send, keep), landed = refs[:5], refs[5:7], refs[7:12]
    halves, arrived = refs[12:]
    loads = [pltpu.make_async_copy(s, d, arrived.at[i]) for i, (s, d) in enumerate(zip(sources, landed))]
    for load in loads:
        load.start()
    q, a_h, a_in, m_h, m_in = landed
    feats = a_in.shape[1]
    loads[0].wait()

    def share(part, first, rows, base):
        for p in range(2 * rows // R):
            g = rank_dot(q[first + p].T, part[p * R : (p + 1) * R] * scale)
            for i in range(R // 8):
                half, local = divmod(p * R + i * 8, rows)
                for c in range(feats // 128):
                    at = (base + local) // 8 * (feats // 128) + c
                    halves[half, at] = g[i * 8 : i * 8 + 8, c * 128 : c * 128 + 128]

    loads[1].wait()
    loads[2].wait()
    part = lax.dot_general(a_h[...], a_in[...], (((1,), (0,)), ((), ())), preferred_element_type=F32)
    share(part, 0, HALF_A, 0)
    loads[3].wait()
    loads[4].wait()
    part = lax.dot_general(m_h[...], m_in[...], (((0,), (0,)), ((), ())), preferred_element_type=F32)
    share(part, CA // R, HALF_M, HALF_A)
    core = lax.axis_index("dp") % 2
    send[...] = halves[1 - core]
    keep[...] = halves[core]


def core_add_kernel(keep, both, out):
    core = lax.axis_index("dp") % 2
    out[...] = keep[...] + both[1 - core]


def rows_of(tiles, rows, first=0):
    cts = tiles.shape[0] // (HALF // 8)
    return jnp.concatenate(
        [
            jnp.concatenate([tiles[(first + r) * cts + c] for c in range(cts)], axis=1)
            for r in range(rows // 8)
        ]
    )


def sum_kernel(got, out):
    out[...] = (got[0] + got[1]) + (got[2] + got[3])


def add_kernel(one, two, out):
    out[...] = one[...] + two[...]


def rotate_kernel(pre, basis, out):
    feats, cts = basis.shape[0] // 2, basis.shape[1] // 128
    rot_a = exact_dot(rows_of(pre, HALF_A), basis[:feats], 0)
    rot_m = exact_dot(rows_of(pre, HALF_M, HALF_A // 8), basis[feats:], 0)
    for y in range(4):
        for rot, count, first, base in ((rot_a, Y_A // 8, y * Y_A, 0), (rot_m, Y_M // 8, y * Y_M, Y_A // 8)):
            for i in range(count):
                row = first + i * 8
                for c in range(cts):
                    out[y, (base + i) * cts + c] = rot[row : row + 8, c * 128 : c * 128 + 128]


def scale_kernel(one, two, own, other, eig, out):
    core = lax.axis_index("dp") % 2
    y = lax.axis_index("factor") // 4
    cts = one.shape[0] // ((Y_A + Y_M) // 8)
    eigs = own.shape[0] - cts
    lane = lax.broadcasted_iota(jnp.int32, (8, R), 1)
    sub = lax.broadcasted_iota(jnp.int32, (8, R), 0)
    quad = jnp.zeros((8, 128), F32)
    for rt in range((Y_A + Y_M) // 8):
        if rt < Y_A // 8:
            row, tail = core * HALF_A + y * Y_A + rt * 8, 0
        else:
            row, tail = CA + core * HALF_M + y * Y_M + (rt - Y_A // 8) * 8, cts // 2
        values = jnp.broadcast_to(eig[pl.ds(row // R, 1), :], (8, R))
        col = jnp.sum(jnp.where(lane == sub + row % R, values, 0.0), axis=1, keepdims=True)
        for c in range(cts):
            t = rt * cts + c
            rot = one[t] + two[t]
            source = own if c < cts // 2 else other
            scaled = rot / (col * source[eigs + tail + c % (cts // 2)] + damping)
            quad += scaled * rot
            for k in range(4):
                out[k, t] = scaled
    for k in range(4):
        out[k, out.shape[1] - 1] = quad


def back_kernel(got, basis, out, quad):
    feats = basis.shape[0] // 2
    cts = basis.shape[1] // 128

    def gather(count, base):
        return jnp.concatenate(
            [
                jnp.concatenate([got[y, (base + i) * cts + c] for c in range(cts)], axis=1)
                for y in range(4)
                for i in range(count)
            ]
        )

    back_a = exact_dot(gather(Y_A // 8, 0), basis[:feats], 1)
    back_m = exact_dot(gather(Y_M // 8, Y_A // 8), basis[feats:], 1)
    fts = feats // 128
    per = HALF // 8 * fts // 16
    for back, count, base in ((back_a, HALF_A // 8, 0), (back_m, HALF_M // 8, HALF_A // 8)):
        for i in range(count):
            for c in range(fts):
                t = (base + i) * fts + c
                out[t // per, t % per] = back[i * 8 : i * 8 + 8, c * 128 : c * 128 + 128]
    last = got.shape[1] - 1
    quad[...] = (got[0, last] + got[1, last]) + (got[2, last] + got[3, last])


def share_kernel(got, quad, out):
    total = got[0]
    for k in range(1, got.shape[0]):
        total = total + got[k]
    for k in range(out.shape[0]):
        out[k, : got.shape[1]] = total
        out[k, got.shape[1]] = quad[...]


def final_kernel(both, q, attn, mlp, result, stored):
    per = both.shape[2] - 1
    fts = attn.shape[1] // 128
    quad = both[0, 0, per] + both[1, 0, per]
    for k in range(1, both.shape[1]):
        quad = quad + (both[0, k, per] + both[1, k, per])
    quad = jnp.sum(quad, keepdims=True)
    clip = jnp.minimum(1.0, jnp.sqrt(kl_limit / quad))
    stores = []
    for p in range(ROWS // R):
        rows = []
        for i in range(R // 8):
            row = p * R + i * 8
            if row < CA:
                half, local = divmod(row, HALF_A)
            else:
                half, local = divmod(row - CA, HALF_M)
                local += HALF_A
            ts = [local // 8 * fts + c for c in range(fts)]
            rows.append(jnp.concatenate([both[half, t // per, t % per] for t in ts], axis=1))
        b = jnp.concatenate(rows)
        b = clip * rank_dot(q[p], b)
        result[p] = b
        target = attn.at[p * R : (p + 1) * R] if p * R < CA else mlp.at[p * R - CA : (p + 1) * R - CA]
        stores.append(pltpu.make_async_copy(result.at[p], target, stored.at[p]))
        stores[-1].start()
    for store in stores:
        store.wait()


def body(
    attn_in,
    mlp_in,
    attn_hgrad,
    mlp_hgrad,
    attn_basis,
    mlp_basis,
    attn_eig,
    mlp_eig,
    rank_basis,
    rank_eig,
):
    tokens, feats = attn_in.shape
    cols = attn_basis.shape[1]
    scale = 1.0 / (tokens * lax.axis_size("dp"))
    half_tiles = HALF // 8 * feats // 128
    y_tiles = HALF // 32 * 2 * cols // 128
    basis_tiles = 2 * (feats + 8) // 8 * cols // 128
    sources = (rank_basis, attn_hgrad.T, attn_in, mlp_hgrad, mlp_in)
    send, keep = pl.pallas_call(
        functools.partial(grad_kernel, scale),
        in_specs=[HBM] * len(sources),
        out_specs=[VMEM] * 2,
        out_shape=[shape(half_tiles, 8, 128)] * 2,
        scratch_shapes=[pltpu.VMEM(s.shape, s.dtype) for s in sources]
        + [pltpu.VMEM((2, half_tiles, 8, 128), F32), pltpu.SemaphoreType.DMA((len(sources),))],
        compiler_params=LIMIT,
        name="grad",
    )(*far(*sources))
    both = lax.all_gather(send, "dp", axis_index_groups=CORE_PAIRS)
    part = pl.pallas_call(
        core_add_kernel,
        in_specs=[VMEM] * 2,
        out_specs=VMEM,
        out_shape=shape(half_tiles, 8, 128),
        compiler_params=LIMIT,
        name="core_add",
    )(*near(keep, both))

    part, attn_basis, mlp_basis = lax.optimization_barrier((part, attn_basis, mlp_basis))
    wide = pl.pallas_call(
        widen_kernel,
        in_specs=[VMEM] * 4,
        out_specs=VMEM,
        out_shape=shape(basis_tiles, 8, 128),
        compiler_params=LIMIT,
        name="widen",
    )(*near(attn_basis, mlp_basis, attn_eig.reshape(1, -1), mlp_eig.reshape(1, -1)))
    other = lax.ppermute(wide, "dp", [(i, i ^ 1) for i in range(lax.axis_size("dp"))])
    basis = pl.pallas_call(
        join_kernel,
        in_specs=[VMEM] * 2,
        out_specs=VMEM,
        out_shape=shape(2 * feats, 2 * cols, dtype=BF16),
        compiler_params=LIMIT,
        name="join",
    )(*near(wide, other))
    shard, basis = lax.optimization_barrier((exchange(part.reshape(16, -1, 8, 128), "dp", CHIPS), basis))
    shard = jnp.sum(shard, axis=0)
    pre = exchange(copies(shard, 16), "dp", CHIPS).reshape(-1, 8, 128)

    block = pl.pallas_call(
        rotate_kernel,
        in_specs=[VMEM] * 2,
        out_specs=VMEM,
        out_shape=shape(4, y_tiles, 8, 128),
        compiler_params=LIMIT,
        name="rotate",
    )(*near(pre, basis))
    block = pl.pallas_call(
        sum_kernel,
        in_specs=[VMEM],
        out_specs=VMEM,
        out_shape=shape(y_tiles, 8, 128),
        compiler_params=LIMIT,
        name="y_sum",
    )(*near(exchange(block, "factor", Y_GROUPS)))
    block = pl.pallas_call(
        add_kernel,
        in_specs=[VMEM] * 2,
        out_specs=VMEM,
        out_shape=shape(y_tiles, 8, 128),
        compiler_params=LIMIT,
        name="z_add",
    )(*near(block, lax.ppermute(block, "factor", Z_PAIRS)))
    across = lax.ppermute(block, "factor", Z_CROSS)
    scaled = pl.pallas_call(
        scale_kernel,
        in_specs=[VMEM] * 5,
        out_specs=VMEM,
        out_shape=shape(4, y_tiles + 1, 8, 128),
        compiler_params=LIMIT,
        name="scale",
    )(*near(block, across, wide, other, rank_eig))
    scaled = exchange(scaled, "factor", Y_GROUPS)
    back, quad = pl.pallas_call(
        back_kernel,
        in_specs=[VMEM] * 2,
        out_specs=[VMEM] * 2,
        out_shape=[shape(16, half_tiles // 16, 8, 128), shape(8, 128)],
        compiler_params=LIMIT,
        name="back",
    )(*near(scaled, basis))
    back = pl.pallas_call(
        share_kernel,
        in_specs=[VMEM] * 2,
        out_specs=VMEM,
        out_shape=shape(16, half_tiles // 16 + 1, 8, 128),
        compiler_params=LIMIT,
        name="share",
    )(*near(exchange(back, "dp", CHIPS), quad))
    back = exchange(back, "dp", CHIPS)
    both = lax.all_gather(back, "dp", axis_index_groups=CORE_PAIRS)
    return tuple(
        pl.pallas_call(
            final_kernel,
            in_specs=[VMEM] * 2,
            out_specs=[HBM] * 2,
            scratch_shapes=[pltpu.VMEM((ROWS // R, R, feats), F32), pltpu.SemaphoreType.DMA((ROWS // R,))],
            compiler_params=LIMIT,
            out_shape=[jax.ShapeDtypeStruct((CA, feats), F32), jax.ShapeDtypeStruct((CM, feats), F32)],
            name="final",
        )(*near(both, rank_basis))
    )


def solution(mesh):
    in_specs = (
        P("dp", "factor"),
        P("dp", "factor"),
        P("dp", None),
        P("dp", None),
        P("factor", "dp"),
        P("factor", "dp"),
        P("dp"),
        P("dp"),
        P(),
        P(),
    )
    out_specs = (P(None, "factor"), P(None, "factor"))

    return jax.shard_map(body, mesh=mesh, in_specs=in_specs, out_specs=out_specs, check_vma=False)
```

```python
import functools

import jax
import jax.numpy as jnp
from jax import lax
from jax.experimental import pallas as pl
from jax.experimental.pallas import tpu as pltpu
from jax.sharding import PartitionSpec as P

damping = 0.001
kl_limit = 8000.0
F32, BF16 = jnp.float32, jnp.bfloat16

CORE_PAIRS = [[x * 8 + z * 2 + c for c in range(2)] for x in range(4) for z in range(4)]
CHIPS = [[x * 8 + (z if x % 2 == 0 else 3 - z) * 2 + c for x in range(4) for z in range(4)] for c in range(2)]
Y_GROUPS = [[y * 4 + z for y in range(4)] for z in range(4)]
Z_PAIRS = [(y * 4 + z, y * 4 + (z ^ 1)) for y in range(4) for z in range(4)]
Z_CROSS = [(y * 4 + z, y * 4 + 3 - z) for y in range(4) for z in range(4)]

CA, CM, R = 192, 128, 64
ROWS, HALF_A, HALF_M = CA + CM, CA // 2, CM // 2
HALF = HALF_A + HALF_M
Y_A, Y_M = HALF_A // 4, HALF_M // 4


def exchange(x, axis, groups):
    return lax.all_to_all(x, axis, 0, 0, axis_index_groups=groups, tiled=True)


def copies(x, count):
    return jnp.broadcast_to(x[None], (count,) + x.shape)


def shape(*dims, dtype=F32):
    return pltpu.VMEM(dims, dtype)


def far(*arrays):
    return [pltpu.with_memory_space_constraint(a, pltpu.HBM) for a in arrays]


def near(*arrays):
    return [pltpu.with_memory_space_constraint(a, pltpu.VMEM) for a in arrays]


LIMIT = pltpu.CompilerParams(vmem_limit_bytes=12 * 2**20)
VMEM = pl.BlockSpec(memory_space=pltpu.VMEM)
HBM = pl.BlockSpec(memory_space=pltpu.HBM)


def pieces(x):
    a = x.astype(BF16)
    r = x - a.astype(F32)
    b = r.astype(BF16)
    return a, b, (r - b.astype(F32)).astype(BF16)


def exact_dot(x, basis, contract):
    n = x.shape[0]
    stacked = jnp.concatenate(pieces(x), axis=0)
    out = lax.dot_general(stacked, basis, (((1,), (contract,)), ((), ())), preferred_element_type=F32)
    return (out[2 * n :] + out[n : 2 * n]) + out[:n]


def rank_dot(blocks, x):
    qa, qb, _ = pieces(blocks)
    a, b, _ = pieces(x)
    left = jnp.concatenate([qb, qa, qb, qa], axis=1)
    right = jnp.concatenate([b, b, a, a], axis=0)
    return lax.dot_general(left, right, (((1,), (0,)), ((), ())), preferred_element_type=F32)


def widen_kernel(a_b, m_b, a_eig, m_eig, wide):
    t = 0
    feats, cols = a_b.shape
    for basis in (a_b, m_b):
        for r in range(0, feats, 16):
            block = basis[r : r + 16].astype(F32)
            for k in range(2):
                for c in range(cols // 128):
                    wide[t] = block[k * 8 : k * 8 + 8, c * 128 : c * 128 + 128]
                    t += 1
    for eig in (a_eig, m_eig):
        for c in range(cols // 128):
            wide[t] = jnp.broadcast_to(eig[:, c * 128 : c * 128 + 128], (8, 128))
            t += 1


def join_kernel(own, other, basis):
    rows, cols = basis.shape
    cts = cols // 256
    for side, source in enumerate((own, other)):
        for r in range(0, rows, 16):
            t = r // 8 * cts
            for c in range(cts):
                pair = jnp.concatenate([source[t + c], source[t + cts + c]])
                basis[r : r + 16, (side * cts + c) * 128 : (side * cts + c + 1) * 128] = pair.astype(BF16)


def grad_kernel(scale, *refs):
    sources, (send, keep), landed = refs[:5], refs[5:7], refs[7:12]
    halves, arrived = refs[12:]
    loads = [pltpu.make_async_copy(s, d, arrived.at[i]) for i, (s, d) in enumerate(zip(sources, landed))]
    for load in loads:
        load.start()
    q, a_h, a_in, m_h, m_in = landed
    feats = a_in.shape[1]
    loads[0].wait()

    def share(part, first, rows, base):
        for p in range(2 * rows // R):
            g = rank_dot(q[first + p].T, part[p * R : (p + 1) * R] * scale)
            for i in range(R // 8):
                half, local = divmod(p * R + i * 8, rows)
                for c in range(feats // 128):
                    at = (base + local) // 8 * (feats // 128) + c
                    halves[half, at] = g[i * 8 : i * 8 + 8, c * 128 : c * 128 + 128]

    loads[1].wait()
    loads[2].wait()
    part = lax.dot_general(a_h[...], a_in[...], (((1,), (0,)), ((), ())), preferred_element_type=F32)
    share(part, 0, HALF_A, 0)
    loads[3].wait()
    loads[4].wait()
    part = lax.dot_general(m_h[...], m_in[...], (((0,), (0,)), ((), ())), preferred_element_type=F32)
    share(part, CA // R, HALF_M, HALF_A)
    core = lax.axis_index("dp") % 2
    send[...] = halves[1 - core]
    keep[...] = halves[core]


def core_add_kernel(keep, both, out):
    core = lax.axis_index("dp") % 2
    out[...] = keep[...] + both[1 - core]


def rows_of(tiles, rows, first=0):
    cts = tiles.shape[0] // (HALF // 8)
    return jnp.concatenate(
        [
            jnp.concatenate([tiles[(first + r) * cts + c] for c in range(cts)], axis=1)
            for r in range(rows // 8)
        ]
    )


def sum_kernel(got, out):
    out[...] = (got[0] + got[1]) + (got[2] + got[3])


def add_kernel(one, two, out):
    out[...] = one[...] + two[...]


def rotate_kernel(pre, basis, out):
    feats, cts = basis.shape[0] // 2, basis.shape[1] // 128
    rot_a = exact_dot(rows_of(pre, HALF_A), basis[:feats], 0)
    rot_m = exact_dot(rows_of(pre, HALF_M, HALF_A // 8), basis[feats:], 0)
    for y in range(4):
        for rot, count, first, base in ((rot_a, Y_A // 8, y * Y_A, 0), (rot_m, Y_M // 8, y * Y_M, Y_A // 8)):
            for i in range(count):
                row = first + i * 8
                for c in range(cts):
                    out[y, (base + i) * cts + c] = rot[row : row + 8, c * 128 : c * 128 + 128]


def scale_kernel(one, two, own, other, eig, out):
    core = lax.axis_index("dp") % 2
    y = lax.axis_index("factor") // 4
    cts = one.shape[0] // ((Y_A + Y_M) // 8)
    eigs = own.shape[0] - cts
    lane = lax.broadcasted_iota(jnp.int32, (8, R), 1)
    sub = lax.broadcasted_iota(jnp.int32, (8, R), 0)
    quad = jnp.zeros((8, 128), F32)
    for rt in range((Y_A + Y_M) // 8):
        if rt < Y_A // 8:
            row, tail = core * HALF_A + y * Y_A + rt * 8, 0
        else:
            row, tail = CA + core * HALF_M + y * Y_M + (rt - Y_A // 8) * 8, cts // 2
        values = jnp.broadcast_to(eig[pl.ds(row // R, 1), :], (8, R))
        col = jnp.sum(jnp.where(lane == sub + row % R, values, 0.0), axis=1, keepdims=True)
        for c in range(cts):
            t = rt * cts + c
            rot = one[t] + two[t]
            source = own if c < cts // 2 else other
            scaled = rot / (col * source[eigs + tail + c % (cts // 2)] + damping)
            quad += scaled * rot
            for k in range(4):
                out[k, t] = scaled
    for k in range(4):
        out[k, out.shape[1] - 1] = quad


def back_kernel(got, basis, out, quad):
    feats = basis.shape[0] // 2
    cts = basis.shape[1] // 128

    def gather(count, base):
        return jnp.concatenate(
            [
                jnp.concatenate([got[y, (base + i) * cts + c] for c in range(cts)], axis=1)
                for y in range(4)
                for i in range(count)
            ]
        )

    back_a = exact_dot(gather(Y_A // 8, 0), basis[:feats], 1)
    back_m = exact_dot(gather(Y_M // 8, Y_A // 8), basis[feats:], 1)
    fts = feats // 128
    per = HALF // 8 * fts // 16
    for back, count, base in ((back_a, HALF_A // 8, 0), (back_m, HALF_M // 8, HALF_A // 8)):
        for i in range(count):
            for c in range(fts):
                t = (base + i) * fts + c
                out[t // per, t % per] = back[i * 8 : i * 8 + 8, c * 128 : c * 128 + 128]
    last = got.shape[1] - 1
    quad[...] = (got[0, last] + got[1, last]) + (got[2, last] + got[3, last])


def share_kernel(got, quad, out):
    total = got[0]
    for k in range(1, got.shape[0]):
        total = total + got[k]
    for k in range(out.shape[0]):
        out[k, : got.shape[1]] = total
        out[k, got.shape[1]] = quad[...]


def final_kernel(both, q, attn, mlp, result, stored):
    per = both.shape[2] - 1
    fts = attn.shape[1] // 128
    quad = both[0, 0, per] + both[1, 0, per]
    for k in range(1, both.shape[1]):
        quad = quad + (both[0, k, per] + both[1, k, per])
    quad = jnp.sum(quad, keepdims=True)
    clip = jnp.minimum(1.0, jnp.sqrt(kl_limit / quad))
    stores = []
    for p in range(ROWS // R):
        rows = []
        for i in range(R // 8):
            row = p * R + i * 8
            if row < CA:
                half, local = divmod(row, HALF_A)
            else:
                half, local = divmod(row - CA, HALF_M)
                local += HALF_A
            ts = [local // 8 * fts + c for c in range(fts)]
            rows.append(jnp.concatenate([both[half, t // per, t % per] for t in ts], axis=1))
        b = jnp.concatenate(rows)
        b = clip * rank_dot(q[p], b)
        result[p] = b
        target = attn.at[p * R : (p + 1) * R] if p * R < CA else mlp.at[p * R - CA : (p + 1) * R - CA]
        stores.append(pltpu.make_async_copy(result.at[p], target, stored.at[p]))
        stores[-1].start()
    for store in stores:
        store.wait()


def body(
    attn_in,
    mlp_in,
    attn_hgrad,
    mlp_hgrad,
    attn_basis,
    mlp_basis,
    attn_eig,
    mlp_eig,
    rank_basis,
    rank_eig,
):
    tokens, feats = attn_in.shape
    cols = attn_basis.shape[1]
    scale = 1.0 / (tokens * lax.axis_size("dp"))
    half_tiles = HALF // 8 * feats // 128
    y_tiles = HALF // 32 * 2 * cols // 128
    basis_tiles = 2 * (feats + 8) // 8 * cols // 128
    sources = (rank_basis, attn_hgrad.T, attn_in, mlp_hgrad, mlp_in)
    send, keep = pl.pallas_call(
        functools.partial(grad_kernel, scale),
        in_specs=[HBM] * len(sources),
        out_specs=[VMEM] * 2,
        out_shape=[shape(half_tiles, 8, 128)] * 2,
        scratch_shapes=[pltpu.VMEM(s.shape, s.dtype) for s in sources]
        + [pltpu.VMEM((2, half_tiles, 8, 128), F32), pltpu.SemaphoreType.DMA((len(sources),))],
        compiler_params=LIMIT,
        name="grad",
    )(*far(*sources))
    both = lax.all_gather(send, "dp", axis_index_groups=CORE_PAIRS)
    part = pl.pallas_call(
        core_add_kernel,
        in_specs=[VMEM] * 2,
        out_specs=VMEM,
        out_shape=shape(half_tiles, 8, 128),
        compiler_params=LIMIT,
        name="core_add",
    )(*near(keep, both))

    part, attn_basis, mlp_basis = lax.optimization_barrier((part, attn_basis, mlp_basis))
    wide = pl.pallas_call(
        widen_kernel,
        in_specs=[VMEM] * 4,
        out_specs=VMEM,
        out_shape=shape(basis_tiles, 8, 128),
        compiler_params=LIMIT,
        name="widen",
    )(*near(attn_basis, mlp_basis, attn_eig.reshape(1, -1), mlp_eig.reshape(1, -1)))
    other = lax.ppermute(wide, "dp", [(i, i ^ 1) for i in range(lax.axis_size("dp"))])
    basis = pl.pallas_call(
        join_kernel,
        in_specs=[VMEM] * 2,
        out_specs=VMEM,
        out_shape=shape(2 * feats, 2 * cols, dtype=BF16),
        compiler_params=LIMIT,
        name="join",
    )(*near(wide, other))
    shard, basis = lax.optimization_barrier((exchange(part.reshape(16, -1, 8, 128), "dp", CHIPS), basis))
    shard = jnp.sum(shard, axis=0)
    pre = exchange(copies(shard, 16), "dp", CHIPS).reshape(-1, 8, 128)

    block = pl.pallas_call(
        rotate_kernel,
        in_specs=[VMEM] * 2,
        out_specs=VMEM,
        out_shape=shape(4, y_tiles, 8, 128),
        compiler_params=LIMIT,
        name="rotate",
    )(*near(pre, basis))
    block = pl.pallas_call(
        sum_kernel,
        in_specs=[VMEM],
        out_specs=VMEM,
        out_shape=shape(y_tiles, 8, 128),
        compiler_params=LIMIT,
        name="y_sum",
    )(*near(exchange(block, "factor", Y_GROUPS)))
    block = pl.pallas_call(
        add_kernel,
        in_specs=[VMEM] * 2,
        out_specs=VMEM,
        out_shape=shape(y_tiles, 8, 128),
        compiler_params=LIMIT,
        name="z_add",
    )(*near(block, lax.ppermute(block, "factor", Z_PAIRS)))
    across = lax.ppermute(block, "factor", Z_CROSS)
    scaled = pl.pallas_call(
        scale_kernel,
        in_specs=[VMEM] * 5,
        out_specs=VMEM,
        out_shape=shape(4, y_tiles + 1, 8, 128),
        compiler_params=LIMIT,
        name="scale",
    )(*near(block, across, wide, other, rank_eig))
    scaled = exchange(scaled, "factor", Y_GROUPS)
    back, quad = pl.pallas_call(
        back_kernel,
        in_specs=[VMEM] * 2,
        out_specs=[VMEM] * 2,
        out_shape=[shape(16, half_tiles // 16, 8, 128), shape(8, 128)],
        compiler_params=LIMIT,
        name="back",
    )(*near(scaled, basis))
    back = pl.pallas_call(
        share_kernel,
        in_specs=[VMEM] * 2,
        out_specs=VMEM,
        out_shape=shape(16, half_tiles // 16 + 1, 8, 128),
        compiler_params=LIMIT,
        name="share",
    )(*near(exchange(back, "dp", CHIPS), quad))
    back = exchange(back, "dp", CHIPS)
    both = lax.all_gather(back, "dp", axis_index_groups=CORE_PAIRS)
    return tuple(
        pl.pallas_call(
            final_kernel,
            in_specs=[VMEM] * 2,
            out_specs=[HBM] * 2,
            scratch_shapes=[pltpu.VMEM((ROWS // R, R, feats), F32), pltpu.SemaphoreType.DMA((ROWS // R,))],
            compiler_params=LIMIT,
            out_shape=[jax.ShapeDtypeStruct((CA, feats), F32), jax.ShapeDtypeStruct((CM, feats), F32)],
            name="final",
        )(*near(both, rank_basis))
    )


def solution(mesh):
    in_specs = (
        P("dp", "factor"),
        P("dp", "factor"),
        P("dp", None),
        P("dp", None),
        P("factor", "dp"),
        P("factor", "dp"),
        P("dp"),
        P("dp"),
        P(),
        P(),
    )
    out_specs = (P(None, "factor"), P(None, "factor"))

    return jax.shard_map(body, mesh=mesh, in_specs=in_specs, out_specs=out_specs, check_vma=False)
```

```python
import functools

import jax
import jax.numpy as jnp
from jax import lax
from jax.experimental import pallas as pl
from jax.experimental.pallas import tpu as pltpu
from jax.sharding import PartitionSpec as P

damping = 0.001
kl_limit = 8000.0
F32, BF16 = jnp.float32, jnp.bfloat16

CORE_PAIRS = [[x * 8 + z * 2 + c for c in range(2)] for x in range(4) for z in range(4)]
CHIPS = [[x * 8 + (z if x % 2 == 0 else 3 - z) * 2 + c for x in range(4) for z in range(4)] for c in range(2)]
Y_GROUPS = [[y * 4 + z for y in range(4)] for z in range(4)]
Z_PAIRS = [(y * 4 + z, y * 4 + (z ^ 1)) for y in range(4) for z in range(4)]
Z_CROSS = [(y * 4 + z, y * 4 + 3 - z) for y in range(4) for z in range(4)]

CA, CM, R = 192, 128, 64
ROWS, HALF_A, HALF_M = CA + CM, CA // 2, CM // 2
HALF = HALF_A + HALF_M
Y_A, Y_M = HALF_A // 4, HALF_M // 4


def exchange(x, axis, groups):
    return lax.all_to_all(x, axis, 0, 0, axis_index_groups=groups, tiled=True)


def copies(x, count):
    return jnp.broadcast_to(x[None], (count,) + x.shape)


def shape(*dims, dtype=F32):
    return pltpu.VMEM(dims, dtype)


def far(*arrays):
    return [pltpu.with_memory_space_constraint(a, pltpu.HBM) for a in arrays]


def near(*arrays):
    return [pltpu.with_memory_space_constraint(a, pltpu.VMEM) for a in arrays]


LIMIT = pltpu.CompilerParams(vmem_limit_bytes=12 * 2**20)
VMEM = pl.BlockSpec(memory_space=pltpu.VMEM)
HBM = pl.BlockSpec(memory_space=pltpu.HBM)


def pieces(x):
    a = x.astype(BF16)
    return a, (x - a.astype(F32)).astype(BF16)


def exact_dot(x, basis, contract):
    n = x.shape[0]
    stacked = jnp.concatenate(pieces(x), axis=0)
    out = lax.dot_general(stacked, basis, (((1,), (contract,)), ((), ())), preferred_element_type=F32)
    return out[n:] + out[:n]


def rank_dot(blocks, x):
    qa, qb = pieces(blocks)
    a, b = pieces(x)
    left = jnp.concatenate([qb, qa, qb, qa], axis=1)
    right = jnp.concatenate([b, b, a, a], axis=0)
    return lax.dot_general(left, right, (((1,), (0,)), ((), ())), preferred_element_type=F32)


def widen_kernel(a_b, m_b, a_eig, m_eig, wide):
    t = 0
    feats, cols = a_b.shape
    for basis in (a_b, m_b):
        for r in range(0, feats, 16):
            block = basis[r : r + 16].astype(F32)
            for k in range(2):
                for c in range(cols // 128):
                    wide[t] = block[k * 8 : k * 8 + 8, c * 128 : c * 128 + 128]
                    t += 1
    for eig in (a_eig, m_eig):
        for c in range(cols // 128):
            wide[t] = jnp.broadcast_to(eig[:, c * 128 : c * 128 + 128], (8, 128))
            t += 1


def join_kernel(own, other, basis):
    rows, cols = basis.shape
    cts = cols // 256
    for side, source in enumerate((own, other)):
        for r in range(0, rows, 16):
            t = r // 8 * cts
            for c in range(cts):
                pair = jnp.concatenate([source[t + c], source[t + cts + c]])
                basis[r : r + 16, (side * cts + c) * 128 : (side * cts + c + 1) * 128] = pair.astype(BF16)


def grad_kernel(scale, *refs):
    sources, (send, keep), landed = refs[:5], refs[5:7], refs[7:12]
    halves, arrived = refs[12:]
    loads = [pltpu.make_async_copy(s, d, arrived.at[i]) for i, (s, d) in enumerate(zip(sources, landed))]
    for load in loads:
        load.start()
    q, a_h, a_in, m_h, m_in = landed
    feats = a_in.shape[1]
    loads[0].wait()

    def share(part, first, rows, base):
        for p in range(2 * rows // R):
            g = rank_dot(q[first + p].T, part[p * R : (p + 1) * R] * scale)
            for i in range(R // 8):
                half, local = divmod(p * R + i * 8, rows)
                for c in range(feats // 128):
                    at = (base + local) // 8 * (feats // 128) + c
                    halves[half, at] = g[i * 8 : i * 8 + 8, c * 128 : c * 128 + 128]

    loads[1].wait()
    loads[2].wait()
    part = lax.dot_general(a_h[...], a_in[...], (((1,), (0,)), ((), ())), preferred_element_type=F32)
    share(part, 0, HALF_A, 0)
    loads[3].wait()
    loads[4].wait()
    part = lax.dot_general(m_h[...], m_in[...], (((0,), (0,)), ((), ())), preferred_element_type=F32)
    share(part, CA // R, HALF_M, HALF_A)
    core = lax.axis_index("dp") % 2
    send[...] = halves[1 - core]
    keep[...] = halves[core]


def core_add_kernel(keep, both, out):
    core = lax.axis_index("dp") % 2
    out[...] = keep[...] + both[1 - core]


def rows_of(tiles, rows, first=0):
    cts = tiles.shape[0] // (HALF // 8)
    return jnp.concatenate(
        [
            jnp.concatenate([tiles[(first + r) * cts + c] for c in range(cts)], axis=1)
            for r in range(rows // 8)
        ]
    )


def sum_kernel(got, out):
    out[...] = (got[0] + got[1]) + (got[2] + got[3])


def add_kernel(one, two, out):
    out[...] = one[...] + two[...]


def rotate_kernel(pre, basis, out):
    feats, cts = basis.shape[0] // 2, basis.shape[1] // 128
    rot_a = exact_dot(rows_of(pre, HALF_A), basis[:feats], 0)
    rot_m = exact_dot(rows_of(pre, HALF_M, HALF_A // 8), basis[feats:], 0)
    for y in range(4):
        for rot, count, first, base in ((rot_a, Y_A // 8, y * Y_A, 0), (rot_m, Y_M // 8, y * Y_M, Y_A // 8)):
            for i in range(count):
                row = first + i * 8
                for c in range(cts):
                    out[y, (base + i) * cts + c] = rot[row : row + 8, c * 128 : c * 128 + 128]


def scale_kernel(one, two, own, other, eig, out):
    core = lax.axis_index("dp") % 2
    y = lax.axis_index("factor") // 4
    cts = one.shape[0] // ((Y_A + Y_M) // 8)
    eigs = own.shape[0] - cts
    lane = lax.broadcasted_iota(jnp.int32, (8, R), 1)
    sub = lax.broadcasted_iota(jnp.int32, (8, R), 0)
    quad = jnp.zeros((8, 128), F32)
    for rt in range((Y_A + Y_M) // 8):
        if rt < Y_A // 8:
            row, tail = core * HALF_A + y * Y_A + rt * 8, 0
        else:
            row, tail = CA + core * HALF_M + y * Y_M + (rt - Y_A // 8) * 8, cts // 2
        values = jnp.broadcast_to(eig[pl.ds(row // R, 1), :], (8, R))
        col = jnp.sum(jnp.where(lane == sub + row % R, values, 0.0), axis=1, keepdims=True)
        for c in range(cts):
            t = rt * cts + c
            rot = one[t] + two[t]
            source = own if c < cts // 2 else other
            scaled = rot / (col * source[eigs + tail + c % (cts // 2)] + damping)
            quad += scaled * rot
            for k in range(4):
                out[k, t] = scaled
    for k in range(4):
        out[k, out.shape[1] - 1] = quad


def back_kernel(got, basis, out, quad):
    feats = basis.shape[0] // 2
    cts = basis.shape[1] // 128

    def gather(count, base):
        return jnp.concatenate(
            [
                jnp.concatenate([got[y, (base + i) * cts + c] for c in range(cts)], axis=1)
                for y in range(4)
                for i in range(count)
            ]
        )

    back_a = exact_dot(gather(Y_A // 8, 0), basis[:feats], 1)
    back_m = exact_dot(gather(Y_M // 8, Y_A // 8), basis[feats:], 1)
    fts = feats // 128
    per = HALF // 8 * fts // 16
    for back, count, base in ((back_a, HALF_A // 8, 0), (back_m, HALF_M // 8, HALF_A // 8)):
        for i in range(count):
            for c in range(fts):
                t = (base + i) * fts + c
                out[t // per, t % per] = back[i * 8 : i * 8 + 8, c * 128 : c * 128 + 128]
    last = got.shape[1] - 1
    quad[...] = (got[0, last] + got[1, last]) + (got[2, last] + got[3, last])


def share_kernel(got, quad, out):
    total = got[0]
    for k in range(1, got.shape[0]):
        total = total + got[k]
    for k in range(out.shape[0]):
        out[k, : got.shape[1]] = total
        out[k, got.shape[1]] = quad[...]


def final_kernel(both, q, attn, mlp, result, stored):
    per = both.shape[2] - 1
    fts = attn.shape[1] // 128
    quad = both[0, 0, per] + both[1, 0, per]
    for k in range(1, both.shape[1]):
        quad = quad + (both[0, k, per] + both[1, k, per])
    quad = jnp.sum(quad, keepdims=True)
    clip = jnp.minimum(1.0, jnp.sqrt(kl_limit / quad))
    stores = []
    for p in range(ROWS // R):
        rows = []
        for i in range(R // 8):
            row = p * R + i * 8
            if row < CA:
                half, local = divmod(row, HALF_A)
            else:
                half, local = divmod(row - CA, HALF_M)
                local += HALF_A
            ts = [local // 8 * fts + c for c in range(fts)]
            rows.append(jnp.concatenate([both[half, t // per, t % per] for t in ts], axis=1))
        b = jnp.concatenate(rows)
        b = clip * rank_dot(q[p], b)
        result[p] = b
        target = attn.at[p * R : (p + 1) * R] if p * R < CA else mlp.at[p * R - CA : (p + 1) * R - CA]
        stores.append(pltpu.make_async_copy(result.at[p], target, stored.at[p]))
        stores[-1].start()
    for store in stores:
        store.wait()


def body(
    attn_in,
    mlp_in,
    attn_hgrad,
    mlp_hgrad,
    attn_basis,
    mlp_basis,
    attn_eig,
    mlp_eig,
    rank_basis,
    rank_eig,
):
    tokens, feats = attn_in.shape
    cols = attn_basis.shape[1]
    scale = 1.0 / (tokens * lax.axis_size("dp"))
    half_tiles = HALF // 8 * feats // 128
    y_tiles = HALF // 32 * 2 * cols // 128
    basis_tiles = 2 * (feats + 8) // 8 * cols // 128
    sources = (rank_basis, attn_hgrad.T, attn_in, mlp_hgrad, mlp_in)
    send, keep = pl.pallas_call(
        functools.partial(grad_kernel, scale),
        in_specs=[HBM] * len(sources),
        out_specs=[VMEM] * 2,
        out_shape=[shape(half_tiles, 8, 128)] * 2,
        scratch_shapes=[pltpu.VMEM(s.shape, s.dtype) for s in sources]
        + [pltpu.VMEM((2, half_tiles, 8, 128), F32), pltpu.SemaphoreType.DMA((len(sources),))],
        compiler_params=LIMIT,
        name="grad",
    )(*far(*sources))
    both = lax.all_gather(send, "dp", axis_index_groups=CORE_PAIRS)
    part = pl.pallas_call(
        core_add_kernel,
        in_specs=[VMEM] * 2,
        out_specs=VMEM,
        out_shape=shape(half_tiles, 8, 128),
        compiler_params=LIMIT,
        name="core_add",
    )(*near(keep, both))

    part, attn_basis, mlp_basis = lax.optimization_barrier((part, attn_basis, mlp_basis))
    wide = pl.pallas_call(
        widen_kernel,
        in_specs=[VMEM] * 4,
        out_specs=VMEM,
        out_shape=shape(basis_tiles, 8, 128),
        compiler_params=LIMIT,
        name="widen",
    )(*near(attn_basis, mlp_basis, attn_eig.reshape(1, -1), mlp_eig.reshape(1, -1)))
    other = lax.ppermute(wide, "dp", [(i, i ^ 1) for i in range(lax.axis_size("dp"))])
    basis = pl.pallas_call(
        join_kernel,
        in_specs=[VMEM] * 2,
        out_specs=VMEM,
        out_shape=shape(2 * feats, 2 * cols, dtype=BF16),
        compiler_params=LIMIT,
        name="join",
    )(*near(wide, other))
    shard, basis = lax.optimization_barrier((exchange(part.reshape(16, -1, 8, 128), "dp", CHIPS), basis))
    shard = jnp.sum(shard, axis=0)
    pre = exchange(copies(shard, 16), "dp", CHIPS).reshape(-1, 8, 128)

    block = pl.pallas_call(
        rotate_kernel,
        in_specs=[VMEM] * 2,
        out_specs=VMEM,
        out_shape=shape(4, y_tiles, 8, 128),
        compiler_params=LIMIT,
        name="rotate",
    )(*near(pre, basis))
    block = pl.pallas_call(
        sum_kernel,
        in_specs=[VMEM],
        out_specs=VMEM,
        out_shape=shape(y_tiles, 8, 128),
        compiler_params=LIMIT,
        name="y_sum",
    )(*near(exchange(block, "factor", Y_GROUPS)))
    block = pl.pallas_call(
        add_kernel,
        in_specs=[VMEM] * 2,
        out_specs=VMEM,
        out_shape=shape(y_tiles, 8, 128),
        compiler_params=LIMIT,
        name="z_add",
    )(*near(block, lax.ppermute(block, "factor", Z_CROSS)))
    across = lax.ppermute(block, "factor", Z_PAIRS)
    scaled = pl.pallas_call(
        scale_kernel,
        in_specs=[VMEM] * 5,
        out_specs=VMEM,
        out_shape=shape(4, y_tiles + 1, 8, 128),
        compiler_params=LIMIT,
        name="scale",
    )(*near(block, across, wide, other, rank_eig))
    scaled = exchange(scaled, "factor", Y_GROUPS)
    back, quad = pl.pallas_call(
        back_kernel,
        in_specs=[VMEM] * 2,
        out_specs=[VMEM] * 2,
        out_shape=[shape(16, half_tiles // 16, 8, 128), shape(8, 128)],
        compiler_params=LIMIT,
        name="back",
    )(*near(scaled, basis))
    back = pl.pallas_call(
        share_kernel,
        in_specs=[VMEM] * 2,
        out_specs=VMEM,
        out_shape=shape(16, half_tiles // 16 + 1, 8, 128),
        compiler_params=LIMIT,
        name="share",
    )(*near(exchange(back, "dp", CHIPS), quad))
    back = exchange(back, "dp", CHIPS)
    both = lax.all_gather(back, "dp", axis_index_groups=CORE_PAIRS)
    return tuple(
        pl.pallas_call(
            final_kernel,
            in_specs=[VMEM] * 2,
            out_specs=[HBM] * 2,
            scratch_shapes=[pltpu.VMEM((ROWS // R, R, feats), F32), pltpu.SemaphoreType.DMA((ROWS // R,))],
            compiler_params=LIMIT,
            out_shape=[jax.ShapeDtypeStruct((CA, feats), F32), jax.ShapeDtypeStruct((CM, feats), F32)],
            name="final",
        )(*near(both, rank_basis))
    )


def solution(mesh):
    in_specs = (
        P("dp", "factor"),
        P("dp", "factor"),
        P("dp", None),
        P("dp", None),
        P("factor", "dp"),
        P("factor", "dp"),
        P("dp"),
        P("dp"),
        P(),
        P(),
    )
    out_specs = (P(None, "factor"), P(None, "factor"))

    return jax.shard_map(body, mesh=mesh, in_specs=in_specs, out_specs=out_specs, check_vma=False)
```
